512 devices in a mesh: slab: 512 (over z, x, y, core).
Axes of the slice: x: 4, y: 8, z: 8, core: 2. Of those that a mesh axis runs over, the one named last changes fastest.
Arguments:
- krylov_basis_block: float32 [16, 4096, 16, 128], P(None, 'slab'), may hold values from -6 to 6
- companion: float32 [16, 4096, 16, 128], P(None, 'slab'), may hold values from -6 to 6
- region: int32 [4096, 16, 128], P('slab'), may hold values from 0 to 7
- inv_density: float32 [8], replicated, may hold values from 0.3 to 3
- stiffness: float32 [8], replicated, may hold values from 0.5 to 3
- damping: float32 [8], replicated, may hold values from 0.5 to 4
Outputs:
- new_block: float32 [16, 4096, 16, 128], P(None, 'slab')
- projection: float32 [16, 16], replicated
- rfactor: float32 [16, 16], replicated
The draws below stay inside these ranges and needn't reach their ends.
All inputs are finite; a program needn't handle non-finite values.
Results may differ from the reference program's by a relative error of at most 0.00012.
Values sent between devices are 32-bit elements; how exact they have to be, the bound alone decides.
No kernel may reach another device: no remote copies, remote signals or barrier semaphores. Data moves between devices by JAX's collectives and lax.ppermute only.
A program may use at most 64 MiB of HBM per device.

```python
import math
import jax
import jax.numpy as jnp
from jax import lax

KRYLOV_COUNT = 16
REGIONS = 8
NY = 16
NZ = 128
NX = 4096


def place_ends(result, own_key, least, largest):
    longest = result.shape.index(max(result.shape))
    spots = []
    for shift in (0, 1):
        where = [jax.random.randint(jax.random.fold_in(own_key, axis), (), 0, length) for axis, length in enumerate(result.shape)]
        where[longest] = (where[longest] + shift) % result.shape[longest]
        spots.append(tuple(where))
    return result.at[spots[0]].set(least).at[spots[1]].set(largest)


def block_levels(rng, shape, shards, least, high):
    factor_of = 1.0
    for dim, shards_of in shards:
        heights = jax.random.uniform(jax.random.fold_in(jax.random.fold_in(rng, 6), dim), (shards_of,), jnp.float32, least / len(shards), high / len(shards))
        factor_of = factor_of * jnp.repeat(jnp.exp(heights), shape[dim] // shards_of).reshape((-1,) + (1,) * (len(shape) - 1 - dim))
    return factor_of


def normal_values(own_key, extent, width, reach, cuts=(), held_as=jnp.bfloat16):
    gain = block_levels(own_key, extent, cuts, -0.22, 0.18) if cuts else 1.0
    array = jax.random.normal(own_key, extent, jnp.float32) * width * gain
    return jnp.minimum(jnp.maximum(array, -reach), reach).astype(held_as)


def setup_inputs(seed: int = 0) -> dict:
    key_of = jax.random.split(jax.random.key(seed), 7)
    return {
        "krylov_basis_block": normal_values(key_of[0], (KRYLOV_COUNT, NX, NY, NZ), 1.0, 6.0, ((1, 512),), jnp.float32),
        "companion": normal_values(key_of[1], (KRYLOV_COUNT, NX, NY, NZ), 1.0, 6.0, ((1, 512),), jnp.float32),
        "region": place_ends(jax.random.randint(key_of[2], (NX, NY, NZ), 0, REGIONS), jax.random.fold_in(key_of[2], 1), 0, REGIONS - 1).astype(jnp.int32),
        "inv_density": jnp.clip(jnp.exp(jax.random.uniform(key_of[3], (REGIONS,), jnp.float32, math.log(0.3), math.log(3.0))), 0.3, 3.0),
        "stiffness": jnp.clip(jax.random.uniform(key_of[4], (REGIONS,), jnp.float32, 0.5, 3.0), 0.5, 3.0),
        "damping": jnp.clip(jnp.exp(jax.random.uniform(key_of[5], (REGIONS,), jnp.float32, math.log(0.5), math.log(4.0))), 0.5, 4.0),
    }


def lookup(region, table):
    picks = region[None] == jnp.arange(table.shape[0], dtype=jnp.int32)[:, None, None, None]
    return jnp.sum(jnp.where(picks, table[:, None, None, None], jnp.float32(0.0)), axis=0)

def operate(operator_applied, cx, mass, damp, companion):
    padded_basis = jnp.pad(operator_applied, ((0, 0), (0, 0), (1, 1), (1, 1)))
    cpad = jnp.pad(cx, ((0, 0), (1, 1), (1, 1)), mode='edge')
    center_coefficient = padded_basis[:, 1:-1, 1:-1, 1:-1]
    ccenter = cpad[1:-1, 1:-1, 1:-1]
    total = -mass * center_coefficient + damp * companion
    shifts = [(slice(2, None), slice(1, -1), slice(1, -1)), (slice(0, -2), slice(1, -1), slice(1, -1)), (slice(1, -1), slice(2, None), slice(1, -1)), (slice(1, -1), slice(0, -2), slice(1, -1)), (slice(1, -1), slice(1, -1), slice(2, None)), (slice(1, -1), slice(1, -1), slice(0, -2))]
    for selection_mask in shifts:
        neighbour_coefficient = padded_basis[:, selection_mask[0], selection_mask[1], selection_mask[2]]
        bond = 0.5 * (ccenter + cpad[selection_mask])
        total = total + bond * (center_coefficient - neighbour_coefficient)
    return total

def reference(krylov_basis_block, companion, region, inv_density, stiffness, damping):
    coef = lookup(region, inv_density)
    mass = lookup(region, stiffness)
    damp = lookup(region, damping)
    operator_applied = jnp.pad(krylov_basis_block, ((0, 0), (1, 1), (0, 0), (0, 0)))
    cx = jnp.pad(coef, ((1, 1), (0, 0), (0, 0)), mode='edge')
    fresh = operate(operator_applied, cx, mass, damp, companion)
    cell_count = NX * NY * NZ
    basis_matrix = krylov_basis_block.reshape(KRYLOV_COUNT, -1)
    image_matrix = fresh.reshape(KRYLOV_COUNT, -1)
    projection = jnp.dot(basis_matrix, image_matrix.T, precision=lax.Precision.HIGHEST) / cell_count
    reduced_products = image_matrix - jnp.dot(projection.T, basis_matrix, precision=lax.Precision.HIGHEST)
    gram = jnp.dot(reduced_products, reduced_products.T, precision=lax.Precision.HIGHEST) / cell_count
    lower = jnp.linalg.cholesky(gram)
    new_block = lax.linalg.triangular_solve(lower, reduced_products, left_side=True, lower=True)
    return (new_block.reshape(krylov_basis_block.shape), projection, lower.T)
```

```python
import functools

import jax
import jax.numpy as jnp
from jax import lax
from jax.experimental import pallas as pl
from jax.experimental.pallas import tpu as pltpu
from jax.sharding import Mesh
from jax.sharding import PartitionSpec as P

SLAB = ("slab_0", "slab_1", "slab_2", "slab_3")
NV, NX, NY, NZ, NR = 16, 8, 16, 128, 8
CELLS = 4096 * 16 * 128
F32, BF16 = jnp.float32, jnp.bfloat16
SMEM = pl.BlockSpec(memory_space=pltpu.SMEM)
VMEM = pl.BlockSpec(memory_space=pltpu.VMEM)


def table_at(region, table):
    out = jnp.zeros(region.shape, F32)
    for r in range(NR):
        out = jnp.where(region == r, table[r], out)
    return out


def two_parts(x):
    high = x.astype(BF16)
    return high, (x - high.astype(F32)).astype(BF16)


def pack_kernel(core, dens, v_ref, region_ref, out_ref):
    out_ref[0:NV] = v_ref[:, 0]
    out_ref[NV] = table_at(region_ref[0], dens)


def pack(core, side, dens, basis, region):
    def plane(core_ref):
        return (NX - 1) * (1 - core_ref[0]) if side == 0 else (NX - 1) * core_ref[0]

    return pl.pallas_call(
        pack_kernel,
        out_shape=jax.ShapeDtypeStruct((NV + 1, NY, NZ), F32),
        grid_spec=pltpu.PrefetchScalarGridSpec(
            num_scalar_prefetch=1,
            grid=(1,),
            in_specs=[
                SMEM,
                pl.BlockSpec((NV, 1, NY, NZ), lambda g, c: (0, plane(c), 0, 0)),
                pl.BlockSpec((1, NY, NZ), lambda g, c: (plane(c), 0, 0)),
            ],
            out_specs=pl.BlockSpec((NV + 1, NY, NZ), lambda g, c: (0, 0, 0)),
        ),
        compiler_params=pltpu.CompilerParams(vmem_limit_bytes=4 << 20),
        cost_estimate=pl.CostEstimate(flops=1 << 16, bytes_accessed=1 << 18, transcendentals=0),
        name="pack" + str(side),
    )(core, dens, basis, region)


def folded(full):
    rows = lax.broadcasted_iota(jnp.int32, (256, 256), 0)
    cols = lax.broadcasted_iota(jnp.int32, (256, 256), 1)
    kept = jnp.where(rows % 8 == cols % 8, full, 0.0)
    by_row = jnp.sum(kept.reshape(32, 8, 256), axis=1)
    pick = lax.broadcasted_iota(jnp.int32, (256, 128), 0) // 8
    lane = lax.broadcasted_iota(jnp.int32, (256, 128), 1)
    return jnp.dot(by_row, jnp.where(pick == lane, 1.0, 0.0).astype(F32), precision=lax.Precision.HIGHEST)


def products(high, low):
    dims = (((1,), (1,)), ((), ()))
    hh = lax.dot_general(high, high, dims, preferred_element_type=F32)
    hl = lax.dot_general(high, low, dims, preferred_element_type=F32)
    return hh, hl


def main_kernel(dens, stiff, dampt, v_ref, comp_ref, region_ref, x_ref, edge_ref, hh_ref, hl_ref, cx_ref):
    for x in range(NX):
        cx_ref[x] = table_at(region_ref[x], dens)
    yi = lax.broadcasted_iota(jnp.int32, (NY, NZ), 0)
    zi = lax.broadcasted_iota(jnp.int32, (NY, NZ), 1)
    for x in range(NX):
        c = cx_ref[x]
        diag = -table_at(region_ref[x], stiff)
        damp = table_at(region_ref[x], dampt)
        xs = []
        for xn in (x - 1, x + 1):
            if 0 <= xn < NX:
                b = 0.5 * (c + cx_ref[xn])
                diag = diag + b
                xs.append((xn, b))
        sides = []
        for shift, axis, end, at in ((NY - 1, 0, NY - 1, yi), (1, 0, 0, yi), (NZ - 1, 1, NZ - 1, zi), (1, 1, 0, zi)):
            outside = at == end
            b = jnp.where(outside, c, 0.5 * (c + pltpu.roll(c, shift, axis)))
            diag = diag + b
            sides.append((shift, axis, jnp.where(outside, 0.0, b)))

        def one(i, x=x, diag=diag, damp=damp, xs=xs, sides=sides):
            v = v_ref[i, x]
            f = diag * v + damp * comp_ref[i, x]
            for xn, b in xs:
                f = f - b * v_ref[i, xn]
            for shift, axis, b in sides:
                f = f - b * pltpu.roll(v, shift, axis)
            return v, f

        if 0 < x < NX - 1:

            def pair(p, carry, x=x, one=one):
                (v0, f0), (v1, f1) = one(2 * p), one(2 * p + 1)
                rows = pl.multiple_of(16 * p, 16)
                for h in range(2):
                    cols = pl.ds(((x - 1) * 2 + h) * NZ, NZ)
                    s = slice(8 * h, 8 * h + 8)
                    fh, fl = two_parts(jnp.concatenate([f0[s], f1[s]], axis=0))
                    vh, vl = two_parts(jnp.concatenate([v0[s], v1[s]], axis=0))
                    x_ref[pl.ds(rows, 16), cols] = fh
                    x_ref[pl.ds(rows + 128, 16), cols] = vh
                    x_ref[pl.ds(rows + 256, 16), cols] = fl
                    x_ref[pl.ds(rows + 384, 16), cols] = vl
                return carry

            lax.fori_loop(0, NV // 2, pair, 0, unroll=4)
        else:
            e = 0 if x == 0 else 1

            def single(i, carry, e=e, one=one):
                edge_ref[e, i] = one(i)[1]
                return carry

            lax.fori_loop(0, NV, single, 0, unroll=4)
    hh, hl = products(x_ref[0:256], x_ref[256:512])
    hh_ref[...] = hh
    hl_ref[...] = hl


def main(dens, stiff, dampt, basis, companion, region):
    return pl.pallas_call(
        main_kernel,
        out_shape=(
            jax.ShapeDtypeStruct((512, 1536), BF16),
            jax.ShapeDtypeStruct((2, NV, NY, NZ), F32),
            jax.ShapeDtypeStruct((256, 256), F32),
            jax.ShapeDtypeStruct((256, 256), F32),
        ),
        in_specs=[SMEM] * 3 + [VMEM] * 3,
        out_specs=(VMEM,) * 4,
        scratch_shapes=[pltpu.VMEM((NX, NY, NZ), F32)],
        compiler_params=pltpu.CompilerParams(vmem_limit_bytes=16 << 20),
        cost_estimate=pl.CostEstimate(flops=1 << 28, bytes_accessed=5 << 20, transcendentals=0),
        name="main",
    )(dens, stiff, dampt, basis, companion, region)


def edge_kernel(core, edge_ref, hh_ref, hl_ref, own0, own1, got0, got1, x_ref, out_ref):
    upper = (1 - core[0], core[0])
    for side, (own, got) in enumerate(((own0, got0), (own1, got1))):
        place = upper[side]
        c, other = own[NV], got[NV]
        b = 0.5 * (c + jnp.where(other > 0.0, other, c))

        def pair(p, carry, own=own, got=got, place=place, b=b):
            fs, vs = [], []
            for i in (2 * p, 2 * p + 1):
                v = own[i]
                fs.append(edge_ref[place, i] + b * (v - got[i]))
                vs.append(v)
            rows = pl.multiple_of(16 * p, 16)
            for h in range(2):
                cols = pl.ds(pl.multiple_of((place * 2 + h) * NZ, NZ), NZ)
                s = slice(8 * h, 8 * h + 8)
                fh, fl = two_parts(jnp.concatenate([fs[0][s], fs[1][s]], axis=0))
                vh, vl = two_parts(jnp.concatenate([vs[0][s], vs[1][s]], axis=0))
                x_ref[pl.ds(rows, 16), cols] = fh
                x_ref[pl.ds(rows + 128, 16), cols] = vh
                x_ref[pl.ds(rows + 256, 16), cols] = fl
                x_ref[pl.ds(rows + 384, 16), cols] = vl
            return carry

        lax.fori_loop(0, NV // 2, pair, 0, unroll=4)
    hh, hl = products(x_ref[0:256], x_ref[256:512])
    same = folded(hh + hh_ref[...])
    mixed = folded(hl + hl_ref[...])
    eye = jnp.where(
        lax.broadcasted_iota(jnp.int32, (32, 128), 0) == lax.broadcasted_iota(jnp.int32, (32, 128), 1), 1.0, 0.0
    ).astype(F32)
    turned = lax.dot_general(eye, mixed, (((1,), (1,)), ((), ())), precision=lax.Precision.HIGHEST)
    turned = jnp.pad(turned, ((0, 0), (0, 96)))
    total = (same + mixed + turned) * (1.0 / CELLS)
    lanes = total[16:32] + pltpu.roll(total[0:16], 32, 1)
    out_ref[...] = lanes[0:8] + pltpu.roll(lanes[8:16], 64, 1)


def edge(core, edges, hh, hl, own, got):
    return pl.pallas_call(
        edge_kernel,
        out_shape=(jax.ShapeDtypeStruct((512, 512), BF16), jax.ShapeDtypeStruct((8, 128), F32)),
        in_specs=[SMEM] + [VMEM] * 7,
        out_specs=(VMEM, VMEM),
        compiler_params=pltpu.CompilerParams(vmem_limit_bytes=8 << 20),
        cost_estimate=pl.CostEstimate(flops=1 << 27, bytes_accessed=2 << 20, transcendentals=0),
        name="edge",
    )(core, edges, hh, hl, *own, *got)


def finish_kernel(parts_ref, xi_ref, xe_ref, new_ref, proj_ref, r_ref, stage, sems):
    packed = jnp.sum(parts_ref[...], axis=0)
    lanes = jnp.concatenate([packed, pltpu.roll(packed, 64, 1)], axis=0)
    vf, vv, ff, fv = (lanes[:, 16 * k : 16 * k + 16] for k in range(4))
    proj_ref[...] = vf
    exact = functools.partial(jnp.dot, precision=lax.Precision.HIGHEST, preferred_element_type=F32)
    gram = ff + exact(fv, exact(vv, vf) - 2.0 * vf)
    row = lax.broadcasted_iota(jnp.int32, (NV, 128), 0)
    lane = lax.broadcasted_iota(jnp.int32, (NV, 128), 1)
    unit = jnp.where(row + 16 == lane, 1.0, 0.0).astype(F32)
    shifted_fv = jnp.where((lane >= 32) & (lane < 48), pltpu.roll(lanes, 128 - 16, 1), 0.0)
    a = jnp.pad(gram, ((0, 0), (0, 112))) + unit + shifted_fv
    for k in range(NV - 1):
        col = jnp.broadcast_to(a[:, k : k + 1], (NV, 128))
        pivot = jnp.broadcast_to(col[k : k + 1], (NV, 128))
        factor = jnp.where(row > k, col / pivot, 0.0)
        a = a - factor * jnp.broadcast_to(a[k : k + 1], (NV, 128))
    pivots = jnp.sum(jnp.where(row == lane, a, 0.0), axis=1, keepdims=True)
    a = a / jnp.sqrt(pivots)
    r_ref[...] = jnp.where(lane >= row, a, 0.0)[:, 0:NV]
    w = jnp.where(lane < 32, a, -a)
    w = jnp.broadcast_to(w[:, None, :], (NV, 8, 128)).reshape(128, 128)
    wh, wl = two_parts(w)
    source = lax.broadcasted_iota(jnp.int32, (128, 256), 0)
    target = lax.broadcasted_iota(jnp.int32, (128, 256), 1)
    spread = jnp.where(source - 16 == target // 8, 1.0, 0.0).astype(BF16)
    keep = source % 8 == target % 8
    kh, kl = (
        jnp.where(keep, jnp.dot(part, spread, preferred_element_type=F32), 0.0).astype(BF16) for part in (wh, wl)
    )
    khh = jnp.concatenate([kh, kh], axis=1)

    def planes(x_ref, at):
        cols = slice(256 * at, 256 * at + 256)
        return jnp.dot(khh, x_ref[:, cols], preferred_element_type=F32) + jnp.dot(
            kl, x_ref[0:256, cols], preferred_element_type=F32
        )

    copies = []
    for x in range(NX):
        got = planes(xe_ref, 0 if x == 0 else 1) if x in (0, NX - 1) else planes(xi_ref, x - 1)
        for h in range(2):
            stage[:, x, 8 * h : 8 * h + 8, :] = got[:, NZ * h : NZ * h + NZ].reshape(NV, 8, NZ)
        if x % 2:
            pair = pl.ds(x - 1, 2)
            copy = pltpu.make_async_copy(stage.at[:, pair], new_ref.at[:, pair], sems.at[x // 2])
            copy.start()
            copies.append(copy)
    for copy in copies:
        copy.wait()


def finish(parts, xi, xe):
    return pl.pallas_call(
        finish_kernel,
        out_shape=(
            jax.ShapeDtypeStruct((NV, NX, NY, NZ), F32),
            jax.ShapeDtypeStruct((NV, NV), F32),
            jax.ShapeDtypeStruct((NV, NV), F32),
        ),
        in_specs=[VMEM] * 3,
        out_specs=(pl.BlockSpec(memory_space=pl.ANY), VMEM, VMEM),
        scratch_shapes=[pltpu.VMEM((NV, NX, NY, NZ), F32), pltpu.SemaphoreType.DMA((NX // 2,))],
        compiler_params=pltpu.CompilerParams(vmem_limit_bytes=16 << 20),
        cost_estimate=pl.CostEstimate(flops=1 << 29, bytes_accessed=3 << 20, transcendentals=0),
        name="finish",
    )(parts, xi, xe)


def sent_to_all(x, axes):
    peers = lax.axis_size(axes)
    return lax.all_to_all(jnp.broadcast_to(x[None], (peers, *x.shape)), axes, 0, 0, tiled=True)


def shards(krylov_basis_block, companion, region, inv_density, stiffness, damping):
    core = lax.axis_index("slab_3").astype(jnp.int32).reshape(1)
    count = lax.axis_size(SLAB)
    own = [pack(core, side, inv_density, krylov_basis_block, region) for side in (0, 1)]
    pairs = [(i, i ^ 1) for i in range(count)]
    across = [(i, i + 1 if i % 2 else i - 1) for i in range(1, count - 1)]
    got1 = lax.ppermute(own[1], SLAB, across)
    got0 = lax.ppermute(own[0], SLAB, pairs)
    xi, edges, hh, hl = main(inv_density, stiffness, damping, krylov_basis_block, companion, region)
    xe, packed = edge(core, edges, hh, hl, own, (got0, got1))
    near = sent_to_all(packed.reshape(1, 1024), ("slab_1", "slab_2")).sum(axis=0)
    far = sent_to_all(near.reshape(1, 1024), ("slab_0", "slab_3"))
    new_block, projection, rfactor = finish(far.reshape(-1, 8, 128), xi, xe)
    return new_block, projection, rfactor


def solution(mesh):
    torus = Mesh(mesh.devices.reshape(8, 4, 8, 2), SLAB)
    placed = (
        P(None, SLAB, None, None),
        P(None, SLAB, None, None),
        P(SLAB, None, None),
        P(),
        P(),
        P(),
    )
    return jax.shard_map(
        shards,
        mesh=torus,
        in_specs=placed,
        out_specs=(P(None, SLAB, None, None), P(), P()),
        check_vma=False,
    )
```

```python
import functools

import jax
import jax.numpy as jnp
from jax import lax
from jax.experimental import pallas as pl
from jax.experimental.pallas import tpu as pltpu
from jax.sharding import Mesh
from jax.sharding import PartitionSpec as P

SLAB = ("slab_0", "slab_1", "slab_2", "slab_3")
NV, NX, NY, NZ, NR = 16, 8, 16, 128, 8
CELLS = 4096 * 16 * 128
F32, BF16 = jnp.float32, jnp.bfloat16
UNROLL = 4
SMEM = pl.BlockSpec(memory_space=pltpu.SMEM)
VMEM = pl.BlockSpec(memory_space=pltpu.VMEM)


def two_parts(x):
    high = x.astype(BF16)
    return high, (x - high.astype(F32)).astype(BF16)


HBM = pl.BlockSpec(memory_space=pltpu.HBM)


def in_hbm(*arrays):
    return [pltpu.with_memory_space_constraint(a, pltpu.HBM) for a in arrays]


def pack_kernel(core, dens_ref, stiff_ref, damp_ref, v_ref, region_ref, out0, out1, fields, tables, regions, sems):
    outs = (out0, out1)
    at = ((NX - 1) * core[0], (NX - 1) * (1 - core[0]))
    whole = pltpu.make_async_copy(region_ref, regions, sems.at[0])
    small = [
        pltpu.make_async_copy(ref, tables.at[k], sems.at[1 + k]) for k, ref in enumerate((dens_ref, stiff_ref, damp_ref))
    ]
    planes = [pltpu.make_async_copy(v_ref.at[:, at[k]], outs[k].at[pl.ds(0, NV)], sems.at[4 + k]) for k in (0, 1)]
    for copy in (whole, *small, *planes):
        copy.start()
    for copy in (*small, whole):
        copy.wait()
    for x in range(NX):
        region = regions[x]
        values = [jnp.zeros(region.shape, F32)] * 3
        for r in range(NR):
            here = region == r
            values = [jnp.where(here, tables[k, r], values[k]) for k in range(3)]
        for k in range(3):
            fields[k, x] = values[k]
    for k in (0, 1):
        outs[k][NV] = fields[0, at[k]]
    for copy in planes:
        copy.wait()


def pack(core, dens, stiff, dampt, basis, region):
    plane = jax.ShapeDtypeStruct((NV + 1, NY, NZ), F32)
    return pl.pallas_call(
        pack_kernel,
        out_shape=(plane, plane, jax.ShapeDtypeStruct((3, NX, NY, NZ), F32)),
        in_specs=[SMEM] + [HBM] * 5,
        out_specs=(VMEM,) * 3,
        scratch_shapes=[
            pltpu.SMEM((3, NR), F32),
            pltpu.VMEM((NX, NY, NZ), jnp.int32),
            pltpu.SemaphoreType.DMA((6,)),
        ],
        compiler_params=pltpu.CompilerParams(vmem_limit_bytes=4 << 20),
        cost_estimate=pl.CostEstimate(flops=1 << 18, bytes_accessed=1 << 19, transcendentals=0),
        name="pack",
    )(core, *in_hbm(dens, stiff, dampt, basis, region))


def folded(full):
    rows = lax.broadcasted_iota(jnp.int32, (256, 256), 0)
    cols = lax.broadcasted_iota(jnp.int32, (256, 256), 1)
    kept = jnp.where(rows % 8 == cols % 8, full, 0.0)
    by_row = jnp.sum(kept.reshape(32, 8, 256), axis=1)
    pick = lax.broadcasted_iota(jnp.int32, (256, 128), 0) // 8
    lane = lax.broadcasted_iota(jnp.int32, (256, 128), 1)
    return jnp.dot(by_row, jnp.where(pick == lane, 1.0, 0.0).astype(F32), precision=lax.Precision.HIGHEST)


def products(high, low):
    dims = (((1,), (1,)), ((), ()))
    hh = lax.dot_general(high, high, dims, preferred_element_type=F32)
    hl = lax.dot_general(high, low, dims, preferred_element_type=F32)
    return hh, hl


def main_kernel(v_ref, fields, comp_hbm, x_ref, edge_ref, hh_ref, hl_ref, comp_ref, sems):
    order = (*range(1, NX - 1), 0, NX - 1)
    copies = {x: pltpu.make_async_copy(comp_hbm.at[:, x], comp_ref.at[:, x], sems.at[x]) for x in order}
    for x in order:
        copies[x].start()
    yi = lax.broadcasted_iota(jnp.int32, (NY, NZ), 0)
    zi = lax.broadcasted_iota(jnp.int32, (NY, NZ), 1)
    for x in range(1, NX - 1):

        def split(p, carry, x=x):
            v0, v1 = v_ref[2 * p, x], v_ref[2 * p + 1, x]
            rows = pl.multiple_of(16 * p, 16)
            for h in range(2):
                cols = pl.ds(((x - 1) * 2 + h) * NZ, NZ)
                s = slice(8 * h, 8 * h + 8)
                vh, vl = two_parts(jnp.concatenate([v0[s], v1[s]], axis=0))
                x_ref[pl.ds(rows + 128, 16), cols] = vh
                x_ref[pl.ds(rows + 384, 16), cols] = vl
            return carry

        lax.fori_loop(0, NV // 2, split, 0, unroll=UNROLL)
    for x in order:
        c = fields[0, x]
        diag = -fields[1, x]
        damp = fields[2, x]
        xs = []
        for xn in (x - 1, x + 1):
            if 0 <= xn < NX:
                b = 0.5 * (c + fields[0, xn])
                diag = diag + b
                xs.append((xn, b))
        sides = []
        for shift, axis, end, at in ((NY - 1, 0, NY - 1, yi), (1, 0, 0, yi), (NZ - 1, 1, NZ - 1, zi), (1, 1, 0, zi)):
            outside = at == end
            b = jnp.where(outside, c, 0.5 * (c + pltpu.roll(c, shift, axis)))
            diag = diag + b
            sides.append((shift, axis, jnp.where(outside, 0.0, b)))

        def one(i, x=x, diag=diag, damp=damp, xs=xs, sides=sides):
            v = v_ref[i, x]
            f = diag * v + damp * comp_ref[i, x]
            for xn, b in xs:
                f = f - b * v_ref[i, xn]
            for shift, axis, b in sides:
                f = f - b * pltpu.roll(v, shift, axis)
            return f

        copies[x].wait()
        if 0 < x < NX - 1:

            def pair(p, carry, x=x, one=one):
                f0, f1 = one(2 * p), one(2 * p + 1)
                rows = pl.multiple_of(16 * p, 16)
                for h in range(2):
                    cols = pl.ds(((x - 1) * 2 + h) * NZ, NZ)
                    s = slice(8 * h, 8 * h + 8)
                    fh, fl = two_parts(jnp.concatenate([f0[s], f1[s]], axis=0))
                    x_ref[pl.ds(rows, 16), cols] = fh
                    x_ref[pl.ds(rows + 256, 16), cols] = fl
                return carry

            lax.fori_loop(0, NV // 2, pair, 0, unroll=UNROLL)
        else:
            e = 0 if x == 0 else 1

            def single(i, carry, e=e, one=one):
                edge_ref[e, i] = one(i)
                return carry

            lax.fori_loop(0, NV, single, 0, unroll=UNROLL)
    hh, hl = products(x_ref[0:256], x_ref[256:512])
    hh_ref[...] = hh
    hl_ref[...] = hl


def main(basis, fields, companion):
    return pl.pallas_call(
        main_kernel,
        out_shape=(
            jax.ShapeDtypeStruct((512, 1536), BF16),
            jax.ShapeDtypeStruct((2, NV, NY, NZ), F32),
            jax.ShapeDtypeStruct((256, 256), F32),
            jax.ShapeDtypeStruct((256, 256), F32),
        ),
        in_specs=[VMEM, VMEM, HBM],
        out_specs=(VMEM,) * 4,
        scratch_shapes=[pltpu.VMEM((NV, NX, NY, NZ), F32), pltpu.SemaphoreType.DMA((NX,))],
        compiler_params=pltpu.CompilerParams(vmem_limit_bytes=16 << 20),
        cost_estimate=pl.CostEstimate(flops=1 << 28, bytes_accessed=5 << 20, transcendentals=0),
        name="main",
    )(basis, fields, *in_hbm(companion))


def edge_kernel(core, edge_ref, hh_ref, hl_ref, own0, own1, got0, got1, x_ref, out_ref):
    upper = (core[0], 1 - core[0])
    for side, (own, got) in enumerate(((own0, got0), (own1, got1))):
        place = upper[side]
        c, other = own[NV], got[NV]
        b = 0.5 * (c + jnp.where(other > 0.0, other, c))

        def pair(p, carry, own=own, got=got, place=place, b=b):
            fs, vs = [], []
            for i in (2 * p, 2 * p + 1):
                v = own[i]
                fs.append(edge_ref[place, i] + b * (v - got[i]))
                vs.append(v)
            rows = pl.multiple_of(16 * p, 16)
            for h in range(2):
                cols = pl.ds(pl.multiple_of((place * 2 + h) * NZ, NZ), NZ)
                s = slice(8 * h, 8 * h + 8)
                fh, fl = two_parts(jnp.concatenate([fs[0][s], fs[1][s]], axis=0))
                vh, vl = two_parts(jnp.concatenate([vs[0][s], vs[1][s]], axis=0))
                x_ref[pl.ds(rows, 16), cols] = fh
                x_ref[pl.ds(rows + 128, 16), cols] = vh
                x_ref[pl.ds(rows + 256, 16), cols] = fl
                x_ref[pl.ds(rows + 384, 16), cols] = vl
            return carry

        lax.fori_loop(0, NV // 2, pair, 0, unroll=4)
    hh, hl = products(x_ref[0:256], x_ref[256:512])
    same = folded(hh + hh_ref[...])
    mixed = folded(hl + hl_ref[...])
    eye = jnp.where(
        lax.broadcasted_iota(jnp.int32, (32, 128), 0) == lax.broadcasted_iota(jnp.int32, (32, 128), 1), 1.0, 0.0
    ).astype(F32)
    turned = lax.dot_general(eye, mixed, (((1,), (1,)), ((), ())), precision=lax.Precision.HIGHEST)
    turned = jnp.pad(turned, ((0, 0), (0, 96)))
    total = (same + mixed + turned) * (1.0 / CELLS)
    lanes = total[16:32] + pltpu.roll(total[0:16], 32, 1)
    out_ref[...] = lanes[0:8] + pltpu.roll(lanes[8:16], 64, 1)


def edge(core, edges, hh, hl, own, got):
    return pl.pallas_call(
        edge_kernel,
        out_shape=(jax.ShapeDtypeStruct((512, 512), BF16), jax.ShapeDtypeStruct((8, 128), F32)),
        in_specs=[SMEM] + [VMEM] * 7,
        out_specs=(VMEM, VMEM),
        compiler_params=pltpu.CompilerParams(vmem_limit_bytes=8 << 20),
        cost_estimate=pl.CostEstimate(flops=1 << 27, bytes_accessed=2 << 20, transcendentals=0),
        name="edge",
    )(core, edges, hh, hl, *own, *got)


def finish_kernel(parts_ref, xi_ref, xe_ref, new_ref, proj_ref, r_ref, stage, sems):
    packed = jnp.sum(parts_ref[...], axis=0)
    lanes = jnp.concatenate([packed, pltpu.roll(packed, 64, 1)], axis=0)
    vf, vv, ff, fv = (lanes[:, 16 * k : 16 * k + 16] for k in range(4))
    proj_ref[...] = vf
    exact = functools.partial(jnp.dot, precision=lax.Precision.HIGHEST, preferred_element_type=F32)
    gram = ff + exact(fv, exact(vv, vf) - 2.0 * vf)
    row = lax.broadcasted_iota(jnp.int32, (NV, 128), 0)
    lane = lax.broadcasted_iota(jnp.int32, (NV, 128), 1)
    unit = jnp.where(row + 16 == lane, 1.0, 0.0).astype(F32)
    shifted_fv = jnp.where((lane >= 32) & (lane < 48), pltpu.roll(lanes, 128 - 16, 1), 0.0)
    a = jnp.pad(gram, ((0, 0), (0, 112))) + unit + shifted_fv
    for k in range(NV - 1):
        col = jnp.broadcast_to(a[:, k : k + 1], (NV, 128))
        pivot = jnp.broadcast_to(col[k : k + 1], (NV, 128))
        factor = jnp.where(row > k, col / pivot, 0.0)
        a = a - factor * jnp.broadcast_to(a[k : k + 1], (NV, 128))
    pivots = jnp.sum(jnp.where(row == lane, a, 0.0), axis=1, keepdims=True)
    a = a / jnp.sqrt(pivots)
    r_ref[...] = jnp.where(lane >= row, a, 0.0)[:, 0:NV]
    w = jnp.where(lane < 32, a, -a)
    w = jnp.broadcast_to(w[:, None, :], (NV, 8, 128)).reshape(128, 128)
    wh, wl = two_parts(w)
    source = lax.broadcasted_iota(jnp.int32, (128, 256), 0)
    target = lax.broadcasted_iota(jnp.int32, (128, 256), 1)
    spread = jnp.where(source - 16 == target // 8, 1.0, 0.0).astype(BF16)
    keep = source % 8 == target % 8
    kh, kl = (
        jnp.where(keep, jnp.dot(part, spread, preferred_element_type=F32), 0.0).astype(BF16) for part in (wh, wl)
    )
    khh = jnp.concatenate([kh, kh], axis=1)

    def planes(x_ref, at):
        cols = slice(256 * at, 256 * at + 256)
        return jnp.dot(khh, x_ref[:, cols], preferred_element_type=F32) + jnp.dot(
            kl, x_ref[0:256, cols], preferred_element_type=F32
        )

    copies = []
    for x in range(NX):
        got = planes(xe_ref, 0 if x == 0 else 1) if x in (0, NX - 1) else planes(xi_ref, x - 1)
        for h in range(2):
            stage[:, x, 8 * h : 8 * h + 8, :] = got[:, NZ * h : NZ * h + NZ].reshape(NV, 8, NZ)
        if x % 2:
            pair = pl.ds(x - 1, 2)
            copy = pltpu.make_async_copy(stage.at[:, pair], new_ref.at[:, pair], sems.at[x // 2])
            copy.start()
            copies.append(copy)
    for copy in copies:
        copy.wait()


def finish(parts, xi, xe):
    return pl.pallas_call(
        finish_kernel,
        out_shape=(
            jax.ShapeDtypeStruct((NV, NX, NY, NZ), F32),
            jax.ShapeDtypeStruct((NV, NV), F32),
            jax.ShapeDtypeStruct((NV, NV), F32),
        ),
        in_specs=[VMEM] * 3,
        out_specs=(pl.BlockSpec(memory_space=pl.ANY), VMEM, VMEM),
        scratch_shapes=[pltpu.VMEM((NV, NX, NY, NZ), F32), pltpu.SemaphoreType.DMA((NX // 2,))],
        compiler_params=pltpu.CompilerParams(vmem_limit_bytes=16 << 20),
        cost_estimate=pl.CostEstimate(flops=1 << 29, bytes_accessed=3 << 20, transcendentals=0),
        name="finish",
    )(parts, xi, xe)


def sent_to_all(x, axes):
    peers = lax.axis_size(axes)
    return lax.all_to_all(jnp.broadcast_to(x[None], (peers, *x.shape)), axes, 0, 0, tiled=True)


def shards(krylov_basis_block, companion, region, inv_density, stiffness, damping):
    core = lax.axis_index("slab_3").astype(jnp.int32).reshape(1)
    count = lax.axis_size(SLAB)
    *own, fields = pack(core, inv_density, stiffness, damping, krylov_basis_block, region)
    pairs = [(i, i ^ 1) for i in range(count)]
    across = [(i, i + 1 if i % 2 else i - 1) for i in range(1, count - 1)]
    got0 = lax.ppermute(own[0], SLAB, across)
    got1 = lax.ppermute(own[1], SLAB, pairs)
    xi, edges, hh, hl = main(krylov_basis_block, fields, companion)
    xe, packed = edge(core, edges, hh, hl, own, (got0, got1))
    near = sent_to_all(packed.reshape(1, 1024), ("slab_1", "slab_2")).sum(axis=0)
    far = sent_to_all(near.reshape(1, 1024), ("slab_0", "slab_3"))
    new_block, projection, rfactor = finish(far.reshape(-1, 8, 128), xi, xe)
    return new_block, projection, rfactor


def solution(mesh):
    torus = Mesh(mesh.devices.reshape(8, 4, 8, 2), SLAB)
    placed = (
        P(None, SLAB, None, None),
        P(None, SLAB, None, None),
        P(SLAB, None, None),
        P(),
        P(),
        P(),
    )
    return jax.shard_map(
        shards,
        mesh=torus,
        in_specs=placed,
        out_specs=(P(None, SLAB, None, None), P(), P()),
        check_vma=False,
    )
```

```python
import functools

import jax
import jax.numpy as jnp
from jax import lax
from jax.experimental import pallas as pl
from jax.experimental.pallas import tpu as pltpu
from jax.sharding import Mesh
from jax.sharding import PartitionSpec as P

SLAB = ("slab_0", "slab_1", "slab_2", "slab_3")
NV, NX, NY, NZ, NR = 16, 8, 16, 128, 8
CELLS = 4096 * 16 * 128
F32, BF16 = jnp.float32, jnp.bfloat16
SMEM = pl.BlockSpec(memory_space=pltpu.SMEM)
VMEM = pl.BlockSpec(memory_space=pltpu.VMEM)


def two_parts(x):
    high = x.astype(BF16)
    return high, (x - high.astype(F32)).astype(BF16)


HBM = pl.BlockSpec(memory_space=pltpu.HBM)


def in_hbm(*arrays):
    return [pltpu.with_memory_space_constraint(a, pltpu.HBM) for a in arrays]


def pack_kernel(core, dens_ref, stiff_ref, damp_ref, v_ref, region_ref, comp_ref, out0, out1, fields, tables, regions, sems):
    outs = (out0, out1)
    at = ((NX - 1) * core[0], (NX - 1) * (1 - core[0]))
    whole = pltpu.make_async_copy(region_ref, regions, sems.at[0])
    small = [
        pltpu.make_async_copy(ref, tables.at[k], sems.at[1 + k]) for k, ref in enumerate((dens_ref, stiff_ref, damp_ref))
    ]
    planes = [pltpu.make_async_copy(v_ref.at[:, at[k]], outs[k].at[pl.ds(0, NV)], sems.at[4 + k]) for k in (0, 1)]
    for copy in (whole, *small, *planes):
        copy.start()
    for copy in (*small, whole):
        copy.wait()
    for x in range(NX):
        region = regions[x]
        values = [jnp.zeros(region.shape, F32)] * 3
        for r in range(NR):
            here = region == r
            values = [jnp.where(here, tables[k, r], values[k]) for k in range(3)]
        for k in range(3):
            fields[k, x] = values[k]
    for k in (0, 1):
        outs[k][NV] = fields[0, at[k]]
    for copy in planes:
        copy.wait()


def pack(core, dens, stiff, dampt, basis, region, companion):
    plane = jax.ShapeDtypeStruct((NV + 1, NY, NZ), F32)
    return pl.pallas_call(
        pack_kernel,
        out_shape=(plane, plane, jax.ShapeDtypeStruct((3, NX, NY, NZ), F32)),
        in_specs=[SMEM] + [HBM] * 6,
        out_specs=(VMEM,) * 3,
        scratch_shapes=[
            pltpu.SMEM((3, NR), F32),
            pltpu.VMEM((NX, NY, NZ), jnp.int32),
            pltpu.SemaphoreType.DMA((6,)),
        ],
        compiler_params=pltpu.CompilerParams(vmem_limit_bytes=4 << 20),
        cost_estimate=pl.CostEstimate(flops=1 << 18, bytes_accessed=1 << 19, transcendentals=0),
        name="pack",
    )(core, *in_hbm(dens, stiff, dampt, basis, region, companion))


def exact(left, right, dims=((1,), (0,))):
    return lax.dot_general(left, right, (dims, ((), ())), precision=lax.Precision.HIGHEST, preferred_element_type=F32)


def iota(shape, axis):
    return lax.broadcasted_iota(jnp.int32, shape, axis)


def ones_where(condition):
    return jnp.where(condition, 1.0, 0.0).astype(F32)


def folded(full):
    kept = jnp.where(iota((256, 256), 0) % 8 == iota((256, 256), 1) % 8, full, 0.0)
    return jnp.sum(kept.reshape(32, 8, 256), axis=1)


def products(high, low):
    dims = (((1,), (1,)), ((), ()))
    hh = lax.dot_general(high, high, dims, preferred_element_type=F32)
    hl = lax.dot_general(high, low, dims, preferred_element_type=F32)
    return hh, hl


def main_kernel(v_ref, fields, comp_ref, x_ref, edge_ref, hh_ref, hl_ref):
    order = (0, NX - 1, *range(1, NX - 1))
    yi = lax.broadcasted_iota(jnp.int32, (NY, NZ), 0)
    zi = lax.broadcasted_iota(jnp.int32, (NY, NZ), 1)
    for x in range(1, NX - 1):

        def split(p, carry, x=x):
            v0, v1 = v_ref[2 * p, x], v_ref[2 * p + 1, x]
            rows = pl.multiple_of(16 * p, 16)
            for h in range(2):
                cols = pl.ds(((x - 1) * 2 + h) * NZ, NZ)
                s = slice(8 * h, 8 * h + 8)
                vh, vl = two_parts(jnp.concatenate([v0[s], v1[s]], axis=0))
                x_ref[pl.ds(rows + 128, 16), cols] = vh
                x_ref[pl.ds(rows + 384, 16), cols] = vl
            return carry

        lax.fori_loop(0, NV // 2, split, 0, unroll=True)
    for x in order:
        c = fields[0, x]
        diag = -fields[1, x]
        damp = fields[2, x]
        xs = []
        for xn in (x - 1, x + 1):
            if 0 <= xn < NX:
                b = 0.5 * (c + fields[0, xn])
                diag = diag + b
                xs.append((xn, b))
        sides = []
        for shift, axis, end, at in ((NY - 1, 0, NY - 1, yi), (1, 0, 0, yi), (NZ - 1, 1, NZ - 1, zi), (1, 1, 0, zi)):
            outside = at == end
            b = jnp.where(outside, c, 0.5 * (c + pltpu.roll(c, shift, axis)))
            diag = diag + b
            sides.append((shift, axis, jnp.where(outside, 0.0, b)))

        def one(i, x=x, diag=diag, damp=damp, xs=xs, sides=sides):
            v = v_ref[i, x]
            f = diag * v + damp * comp_ref[i, x]
            for xn, b in xs:
                f = f - b * v_ref[i, xn]
            for shift, axis, b in sides:
                f = f - b * pltpu.roll(v, shift, axis)
            return f

        if 0 < x < NX - 1:

            def pair(p, carry, x=x, one=one):
                f0, f1 = one(2 * p), one(2 * p + 1)
                rows = pl.multiple_of(16 * p, 16)
                for h in range(2):
                    cols = pl.ds(((x - 1) * 2 + h) * NZ, NZ)
                    s = slice(8 * h, 8 * h + 8)
                    fh, fl = two_parts(jnp.concatenate([f0[s], f1[s]], axis=0))
                    x_ref[pl.ds(rows, 16), cols] = fh
                    x_ref[pl.ds(rows + 256, 16), cols] = fl
                return carry

            lax.fori_loop(0, NV // 2, pair, 0, unroll=True)
        else:
            e = 0 if x == 0 else 1

            def single(i, carry, e=e, one=one):
                edge_ref[e, i] = one(i)
                return carry

            lax.fori_loop(0, NV, single, 0, unroll=True)
    hh, hl = products(x_ref[0:256], x_ref[256:512])
    hh_ref[...] = hh
    hl_ref[...] = hl


def main(basis, fields, companion):
    return pl.pallas_call(
        main_kernel,
        out_shape=(
            jax.ShapeDtypeStruct((512, 1536), BF16),
            jax.ShapeDtypeStruct((2, NV, NY, NZ), F32),
            jax.ShapeDtypeStruct((256, 256), F32),
            jax.ShapeDtypeStruct((256, 256), F32),
        ),
        in_specs=[VMEM] * 3,
        out_specs=(VMEM,) * 4,
        compiler_params=pltpu.CompilerParams(vmem_limit_bytes=16 << 20),
        cost_estimate=pl.CostEstimate(flops=1 << 28, bytes_accessed=5 << 20, transcendentals=0),
        name="main",
    )(basis, fields, companion)


def edge_kernel(core, edge_ref, hh_ref, hl_ref, own0, own1, got0, got1, xi_ref, x_ref, out_ref, kept_ref):
    upper = (core[0], 1 - core[0])
    for side, (own, got) in enumerate(((own0, got0), (own1, got1))):
        place = upper[side]
        c, other = own[NV], got[NV]
        b = 0.5 * (c + jnp.where(other > 0.0, other, c))

        def pair(p, carry, own=own, got=got, place=place, b=b):
            fs, vs = [], []
            for i in (2 * p, 2 * p + 1):
                v = own[i]
                fs.append(edge_ref[place, i] + b * (v - got[i]))
                vs.append(v)
            rows = pl.multiple_of(16 * p, 16)
            for h in range(2):
                cols = pl.ds(pl.multiple_of((place * 2 + h) * NZ, NZ), NZ)
                s = slice(8 * h, 8 * h + 8)
                fh, fl = two_parts(jnp.concatenate([fs[0][s], fs[1][s]], axis=0))
                vh, vl = two_parts(jnp.concatenate([vs[0][s], vs[1][s]], axis=0))
                x_ref[pl.ds(rows, 16), cols] = fh
                x_ref[pl.ds(rows + 128, 16), cols] = vh
                x_ref[pl.ds(rows + 256, 16), cols] = fl
                x_ref[pl.ds(rows + 384, 16), cols] = vl
            return carry

        lax.fori_loop(0, NV // 2, pair, 0, unroll=4)
    hh, hl = products(x_ref[0:256], x_ref[256:512])
    same = folded(hh + hh_ref[...])
    mixed = folded(hl + hl_ref[...])
    both = same + mixed
    repeat = ones_where(iota((128, 128), 0) // 8 == iota((128, 128), 1) % NV)
    square = exact(mixed, ones_where(iota((256, 128), 0) // 8 == iota((256, 128), 1)))
    group, lane = iota((32, 128), 0), iota((32, 128), 1)
    tiles = [
        exact(both[:, 128 * k : 128 * k + 128], repeat)
        + exact(square, ones_where(group - NV * k == lane % NV), ((0,), (0,)))[0:32]
        for k in (0, 1)
    ]
    row, lane = iota((NV, 128), 0), iota((NV, 128), 1)
    fv, ff, vv = tiles[1][0:NV], tiles[0][0:NV], tiles[1][NV:32]
    sums = []
    for m in (fv, jnp.where(lane % NV >= row, ff, vv)):
        m = jnp.where(lane // NV == row % 8, m, 0.0)
        sums += [jnp.sum(m[0:8], axis=0, keepdims=True), jnp.sum(m[8:16], axis=0, keepdims=True)]
    sums.append(jnp.sum(jnp.where(lane == row, vv, 0.0), axis=0, keepdims=True))
    for k, m in enumerate(sums):
        out_ref[k : k + 1] = m * (1.0 / CELLS)


def edge(core, edges, hh, hl, own, got, xi):
    return pl.pallas_call(
        edge_kernel,
        out_shape=(
            jax.ShapeDtypeStruct((512, 512), BF16),
            jax.ShapeDtypeStruct((5, 128), F32),
            jax.ShapeDtypeStruct(xi.shape, xi.dtype),
        ),
        in_specs=[SMEM] + [VMEM] * 7 + [pl.BlockSpec(memory_space=pl.ANY)],
        out_specs=(VMEM, VMEM, pl.BlockSpec(memory_space=pl.ANY)),
        input_output_aliases={8: 2},
        compiler_params=pltpu.CompilerParams(vmem_limit_bytes=8 << 20),
        cost_estimate=pl.CostEstimate(flops=1 << 27, bytes_accessed=2 << 20, transcendentals=0),
        name="edge",
    )(core, edges, hh, hl, *own, *got, xi)


def finish_kernel(parts_ref, xi_ref, xe_ref, new_ref, proj_ref, r_ref, stage, sems):
    row, lane = iota((NV, 128), 0), iota((NV, 128), 1)
    total = [jnp.sum(parts_ref[pl.ds(k, parts_ref.shape[0] // 5, stride=5), :], axis=0, keepdims=True) for k in range(5)]
    mine = lane // NV == row % 8
    spread_out = [
        jnp.where(mine, jnp.where(row < 8, jnp.broadcast_to(lo, (NV, 128)), jnp.broadcast_to(hi, (NV, 128))), 0.0)
        for lo, hi in ((total[0], total[1]), (total[2], total[3]))
    ]
    spread_out = jnp.concatenate(spread_out, axis=0)
    source, target = iota((128, 128), 0), iota((128, 128), 1)
    squares = exact(spread_out, ones_where((source % NV == target % NV) & (target // NV % 2 == 0) & (target < 48)))
    turned = exact(ones_where(lane % NV == row), spread_out, ((1,), (1,)))
    fv, mixed = squares[0:NV, 0:NV], squares[NV:32, 0:NV]
    vf, mixed_t = turned[:, 0:NV], turned[:, NV:32]
    r, c = iota((NV, NV), 0), iota((NV, NV), 1)
    ff = jnp.where(c >= r, mixed, mixed_t)
    own = jnp.broadcast_to(total[4], (NV, 128))[:, 0:NV]
    vv = jnp.where(c < r, mixed, jnp.where(c > r, mixed_t, own))
    proj_ref[...] = vf
    gram = ff + exact(fv, exact(vv, vf) - 2.0 * vf)
    unit = ones_where(row + 16 == lane)
    a = jnp.pad(gram, ((0, 0), (0, 112))) + unit + jnp.where(lane >= 32, squares[0:NV], 0.0)
    for k in range(0, NV - 2, 2):
        col0, col1 = (jnp.broadcast_to(a[:, k + j : k + j + 1], (NV, 128)) for j in (0, 1))
        row0, row1 = (jnp.broadcast_to(a[k + j : k + j + 1], (NV, 128)) for j in (0, 1))
        p, q, t = (jnp.broadcast_to(m, (NV, 128)) for m in (col0[k : k + 1], col1[k : k + 1], col1[k + 1 : k + 2]))
        scale = jnp.where(row > k + 1, 1.0 / (p * t - q * q), 0.0)
        a = a - ((col0 * t - col1 * q) * scale) * row0 - ((col1 * p - col0 * q) * scale) * row1
    above = pltpu.roll(a, 1, 0)
    below_pivot, pivot = (jnp.sum(jnp.where(lane == row - 1, m, 0.0), axis=1, keepdims=True) for m in (a, above))
    odd = row % 2 == 1
    a = a - jnp.where(odd, below_pivot / jnp.where(odd[:, 0:1], pivot, 1.0), 0.0) * above
    pivots = jnp.sum(jnp.where(row == lane, a, 0.0), axis=1, keepdims=True)
    a = a / jnp.sqrt(pivots)
    r_ref[...] = jnp.where(lane >= row, a, 0.0)[:, 0:NV]
    w = jnp.where(lane < 32, a, -a)
    w = jnp.broadcast_to(w[:, None, :], (NV, 8, 128)).reshape(128, 128)
    wh, wl = two_parts(w)
    source, target = iota((128, 256), 0), iota((128, 256), 1)
    spread = jnp.where(source - 16 == target // 8, 1.0, 0.0).astype(BF16)
    keep = source % 8 == target % 8
    kh, kl = (
        jnp.where(keep, jnp.dot(part, spread, preferred_element_type=F32), 0.0).astype(BF16) for part in (wh, wl)
    )
    khh = jnp.concatenate([kh, kh], axis=1)

    def planes(x_ref, at):
        cols = slice(256 * at, 256 * at + 256)
        return jnp.dot(khh, x_ref[:, cols], preferred_element_type=F32) + jnp.dot(
            kl, x_ref[0:256, cols], preferred_element_type=F32
        )

    copies = []
    for x in range(NX):
        got = planes(xe_ref, 0 if x == 0 else 1) if x in (0, NX - 1) else planes(xi_ref, x - 1)
        for h in range(2):
            stage[:, x, 8 * h : 8 * h + 8, :] = got[:, NZ * h : NZ * h + NZ].reshape(NV, 8, NZ)
        copy = pltpu.make_async_copy(stage.at[:, x], new_ref.at[:, x], sems.at[x])
        copy.start()
        copies.append(copy)
    for copy in copies:
        copy.wait()


def finish(parts, xi, xe):
    return pl.pallas_call(
        finish_kernel,
        out_shape=(
            jax.ShapeDtypeStruct((NV, NX, NY, NZ), F32),
            jax.ShapeDtypeStruct((NV, NV), F32),
            jax.ShapeDtypeStruct((NV, NV), F32),
        ),
        in_specs=[VMEM] * 3,
        out_specs=(pl.BlockSpec(memory_space=pl.ANY), VMEM, VMEM),
        scratch_shapes=[pltpu.VMEM((NV, NX, NY, NZ), F32), pltpu.SemaphoreType.DMA((NX,))],
        compiler_params=pltpu.CompilerParams(vmem_limit_bytes=16 << 20),
        cost_estimate=pl.CostEstimate(flops=1 << 29, bytes_accessed=3 << 20, transcendentals=0),
        name="finish",
    )(parts, xi, xe)


def sent_to_all(x, axes):
    peers = lax.axis_size(axes)
    return lax.all_to_all(jnp.broadcast_to(x[None], (peers, *x.shape)), axes, 0, 0, tiled=True)


def shards(krylov_basis_block, companion, region, inv_density, stiffness, damping):
    core = lax.axis_index("slab_3").astype(jnp.int32).reshape(1)
    count = lax.axis_size(SLAB)
    *own, fields = pack(core, inv_density, stiffness, damping, krylov_basis_block, region, companion)
    pairs = [(i, i ^ 1) for i in range(count)]
    across = [(i, i + 1 if i % 2 else i - 1) for i in range(1, count - 1)]
    got0 = lax.ppermute(own[0], SLAB, across)
    got1 = lax.ppermute(own[1], SLAB, pairs)
    xi, edges, hh, hl = main(krylov_basis_block, fields, companion)
    xe, packed, xi = edge(core, edges, hh, hl, own, (got0, got1), xi)
    near = sent_to_all(packed.reshape(1, 640), ("slab_1", "slab_2")).sum(axis=0)
    far = sent_to_all(near.reshape(1, 640), ("slab_0", "slab_3"))
    new_block, projection, rfactor = finish(far.reshape(-1, 128), xi, xe)
    return new_block, projection, rfactor


def solution(mesh):
    torus = Mesh(mesh.devices.reshape(8, 4, 8, 2), SLAB)
    placed = (
        P(None, SLAB, None, None),
        P(None, SLAB, None, None),
        P(SLAB, None, None),
        P(),
        P(),
        P(),
    )
    return jax.shard_map(
        shards,
        mesh=torus,
        in_specs=placed,
        out_specs=(P(None, SLAB, None, None), P(), P()),
        check_vma=False,
    )
```

```python
import functools

import jax
import jax.numpy as jnp
from jax import lax
from jax.experimental import pallas as pl
from jax.experimental.pallas import tpu as pltpu
from jax.sharding import Mesh
from jax.sharding import PartitionSpec as P

SLAB = ("slab_0", "slab_1", "slab_2", "slab_3")
NV, NX, NY, NZ, NR = 16, 8, 16, 128, 8
CELLS = 4096 * 16 * 128
F32, BF16 = jnp.float32, jnp.bfloat16
SMEM = pl.BlockSpec(memory_space=pltpu.SMEM)
VMEM = pl.BlockSpec(memory_space=pltpu.VMEM)


def two_parts(x):
    high = x.astype(BF16)
    return high, (x - high.astype(F32)).astype(BF16)


HBM = pl.BlockSpec(memory_space=pltpu.HBM)


def in_hbm(*arrays):
    return [pltpu.with_memory_space_constraint(a, pltpu.HBM) for a in arrays]


def pack_kernel(core, dens_ref, stiff_ref, damp_ref, v_ref, region_ref, comp_ref, out0, out1, fields, tables, regions, sems):
    outs = (out0, out1)
    at = ((NX - 1) * core[0], (NX - 1) * (1 - core[0]))
    whole = pltpu.make_async_copy(region_ref, regions, sems.at[0])
    small = [
        pltpu.make_async_copy(ref, tables.at[k], sems.at[1 + k]) for k, ref in enumerate((dens_ref, stiff_ref, damp_ref))
    ]
    planes = [pltpu.make_async_copy(v_ref.at[:, at[k]], outs[k].at[pl.ds(0, NV)], sems.at[4 + k]) for k in (0, 1)]
    for copy in (whole, *small, *planes):
        copy.start()
    for copy in (*small, whole):
        copy.wait()
    for x in range(NX):
        region = regions[x]
        values = [jnp.zeros(region.shape, F32)] * 3
        for r in range(NR):
            here = region == r
            values = [jnp.where(here, tables[k, r], values[k]) for k in range(3)]
        for k in range(3):
            fields[k, x] = values[k]
    for k in (0, 1):
        outs[k][NV] = fields[0, at[k]]
    for copy in planes:
        copy.wait()


def pack(core, dens, stiff, dampt, basis, region, companion):
    plane = jax.ShapeDtypeStruct((NV + 1, NY, NZ), F32)
    return pl.pallas_call(
        pack_kernel,
        out_shape=(plane, plane, jax.ShapeDtypeStruct((3, NX, NY, NZ), F32)),
        in_specs=[SMEM] + [HBM] * 6,
        out_specs=(VMEM,) * 3,
        scratch_shapes=[
            pltpu.SMEM((3, NR), F32),
            pltpu.VMEM((NX, NY, NZ), jnp.int32),
            pltpu.SemaphoreType.DMA((6,)),
        ],
        compiler_params=pltpu.CompilerParams(vmem_limit_bytes=4 << 20),
        cost_estimate=pl.CostEstimate(flops=1 << 18, bytes_accessed=1 << 19, transcendentals=0),
        name="pack",
    )(core, *in_hbm(dens, stiff, dampt, basis, region, companion))


def exact(left, right, dims=((1,), (0,))):
    return lax.dot_general(left, right, (dims, ((), ())), precision=lax.Precision.HIGHEST, preferred_element_type=F32)


def iota(shape, axis):
    return lax.broadcasted_iota(jnp.int32, shape, axis)


def ones_where(condition):
    return jnp.where(condition, 1.0, 0.0).astype(F32)


def folded(full):
    rows, cols = full.shape
    kept = jnp.where(iota(full.shape, 0) % 8 == iota(full.shape, 1) % 8, full, 0.0)
    return jnp.sum(kept.reshape(rows // 8, 8, cols), axis=1)


def tiled(half):
    return exact(half, ones_where(iota((128, 128), 0) // 8 == iota((128, 128), 1) % NV))


def beside(square):
    return jnp.pad(square, ((16, 0), (128, 0)))


def times_turned(left, right):
    return lax.dot_general(left, right, (((1,), (1,)), ((), ())), preferred_element_type=F32)


def main_kernel(v_ref, fields, comp_ref, xf_ref, xv_ref, edge_ref, tiles_ref):
    yi = lax.broadcasted_iota(jnp.int32, (NY, NZ), 0)
    zi = lax.broadcasted_iota(jnp.int32, (NY, NZ), 1)
    for x in range(NX):
        for i in range(0, NV, 2):
            v0, v1 = v_ref[i, x], v_ref[i + 1, x]
            for h in range(2):
                cols, half = slice((2 * x + h) * NZ, (2 * x + h + 1) * NZ), slice(8 * h, 8 * h + 8)
                high, low = two_parts(jnp.concatenate([v0[half], v1[half]], axis=0))
                xv_ref[8 * i : 8 * i + 16, cols] = high
                xv_ref[128 + 8 * i : 144 + 8 * i, cols] = low
    for x in (0, NX - 1, *range(1, NX - 1)):
        c = fields[0, x]
        diag = -fields[1, x]
        damp = fields[2, x]
        xs = []
        for xn in (x - 1, x + 1):
            if 0 <= xn < NX:
                b = 0.5 * (c + fields[0, xn])
                diag = diag + b
                xs.append((xn, b))
        sides = []
        for shift, axis, end, at in ((NY - 1, 0, NY - 1, yi), (1, 0, 0, yi), (NZ - 1, 1, NZ - 1, zi), (1, 1, 0, zi)):
            outside = at == end
            b = jnp.where(outside, c, 0.5 * (c + pltpu.roll(c, shift, axis)))
            diag = diag + b
            sides.append((shift, axis, jnp.where(outside, 0.0, b)))

        def one(i, x=x, diag=diag, damp=damp, xs=xs, sides=sides):
            v = v_ref[i, x]
            f = diag * v + damp * comp_ref[i, x]
            for xn, b in xs:
                f = f - b * v_ref[i, xn]
            for shift, axis, b in sides:
                f = f - b * pltpu.roll(v, shift, axis)
            return f

        if x in (0, NX - 1):
            for i in range(NV):
                edge_ref[x // (NX - 1), i] = one(i)
            continue
        for i in range(0, NV, 2):
            f0, f1 = one(i), one(i + 1)
            for h in range(2):
                at = 2 * (x - 1) + h
                cols, half = slice(at * NZ, (at + 1) * NZ), slice(8 * h, 8 * h + 8)
                high, low = two_parts(jnp.concatenate([f0[half], f1[half]], axis=0))
                xf_ref[8 * i : 8 * i + 16, cols] = high
                xf_ref[128 + 8 * i : 144 + 8 * i, cols] = low
    inner, ends = slice(2 * NZ, 14 * NZ), (slice(0, 2 * NZ), slice(14 * NZ, 16 * NZ))
    high, low = (jnp.concatenate([xf_ref[k : k + 128], xv_ref[k : k + 128, inner]], axis=0) for k in (0, 128))
    end_high, end_low = (jnp.concatenate([xv_ref[k : k + 128, e] for e in ends], axis=1) for k in (0, 128))
    same, mixed = (
        folded(times_turned(high, right)) + beside(folded(times_turned(end_high, end_right)))
        for right, end_right in ((high, end_high), (low, end_low))
    )
    both = same + mixed
    square = exact(mixed, ones_where(iota((256, 128), 0) // 8 == iota((256, 128), 1)))
    group, lane = iota((32, 128), 0), iota((32, 128), 1)
    over_f, over_v = (
        tiled(both[:, 128 * k : 128 * k + 128])
        + exact(square, ones_where(group - NV * k == lane % NV), ((0,), (0,)))[0:32]
        for k in (0, 1)
    )
    tiles_ref[0:NV] = over_f[0:NV]
    tiles_ref[NV : NV + 32] = over_v


def main(basis, fields, companion):
    return pl.pallas_call(
        main_kernel,
        out_shape=(
            jax.ShapeDtypeStruct((256, 1536), BF16),
            jax.ShapeDtypeStruct((256, 2048), BF16),
            jax.ShapeDtypeStruct((2, NV, NY, NZ), F32),
            jax.ShapeDtypeStruct((48, 128), F32),
        ),
        in_specs=[VMEM] * 3,
        out_specs=(VMEM,) * 4,
        compiler_params=pltpu.CompilerParams(vmem_limit_bytes=16 << 20),
        cost_estimate=pl.CostEstimate(flops=1 << 28, bytes_accessed=5 << 20, transcendentals=0),
        name="main",
    )(basis, fields, companion)


def edge_kernel(core, edge_ref, tiles_ref, xv_ref, own0, own1, got0, got1, xf_ref, xe_ref, out_ref, kept_ref):
    upper = (core[0], 1 - core[0])
    for side, (own, got) in enumerate(((own0, got0), (own1, got1))):
        place = upper[side]
        c, other = own[NV], got[NV]
        b = 0.5 * (c + jnp.where(other > 0.0, other, c))
        for i in range(0, NV, 2):
            f0, f1 = (edge_ref[place, k] + b * (own[k] - got[k]) for k in (i, i + 1))
            for h in range(2):
                cols, half = pl.ds(pl.multiple_of((place * 2 + h) * NZ, NZ), NZ), slice(8 * h, 8 * h + 8)
                high, low = two_parts(jnp.concatenate([f0[half], f1[half]], axis=0))
                xe_ref[8 * i : 8 * i + 16, cols] = high
                xe_ref[128 + 8 * i : 144 + 8 * i, cols] = low
    fh, fl = xe_ref[0:128], xe_ref[128:256]
    ends = (slice(0, 2 * NZ), slice(14 * NZ, 16 * NZ))
    vh, vl = (jnp.concatenate([xv_ref[k : k + 128, e] for e in ends], axis=1) for k in (0, 128))
    high, low = jnp.concatenate([fh, vh], axis=0), jnp.concatenate([fl, vl], axis=0)
    sums = folded(
        times_turned(jnp.concatenate([fh, fh, fl], axis=1), jnp.concatenate([high, low, high], axis=1))
    )
    ff = tiled(sums[:, 0:128]) + tiles_ref[0:NV]
    fv = tiled(sums[:, 128:256]) + tiles_ref[NV:32]
    vv = tiles_ref[32:48]
    row, lane = iota((NV, 128), 0), iota((NV, 128), 1)
    sums = []
    for m in (fv, jnp.where(lane % NV >= row, ff, vv)):
        m = jnp.where(lane // NV == row % 8, m, 0.0)
        sums += [jnp.sum(m[0:8], axis=0, keepdims=True), jnp.sum(m[8:16], axis=0, keepdims=True)]
    sums.append(jnp.sum(jnp.where(lane == row, vv, 0.0), axis=0, keepdims=True))
    for k, m in enumerate(sums):
        out_ref[k : k + 1] = m * (1.0 / CELLS)


def edge(core, edges, tiles, xv, own, got, xf):
    anywhere = pl.BlockSpec(memory_space=pl.ANY)
    return pl.pallas_call(
        edge_kernel,
        out_shape=(
            jax.ShapeDtypeStruct((256, 512), BF16),
            jax.ShapeDtypeStruct((5, 128), F32),
            jax.ShapeDtypeStruct(xf.shape, xf.dtype),
        ),
        in_specs=[SMEM] + [VMEM] * 7 + [anywhere],
        out_specs=(VMEM, VMEM, anywhere),
        input_output_aliases={8: 2},
        compiler_params=pltpu.CompilerParams(vmem_limit_bytes=8 << 20),
        cost_estimate=pl.CostEstimate(flops=1 << 27, bytes_accessed=2 << 20, transcendentals=0),
        name="edge",
    )(core, edges, tiles, xv, *own, *got, xf)


def finish_kernel(parts_ref, xf_ref, xe_ref, xv_ref, new_ref, proj_ref, r_ref, stage, sems):
    row, lane = iota((NV, 128), 0), iota((NV, 128), 1)
    total = [jnp.sum(parts_ref[pl.ds(k, parts_ref.shape[0] // 5, stride=5), :], axis=0, keepdims=True) for k in range(5)]
    mine = lane // NV == row % 8
    spread_out = [
        jnp.where(mine, jnp.where(row < 8, jnp.broadcast_to(lo, (NV, 128)), jnp.broadcast_to(hi, (NV, 128))), 0.0)
        for lo, hi in ((total[0], total[1]), (total[2], total[3]))
    ]
    spread_out = jnp.concatenate(spread_out, axis=0)
    source, target = iota((128, 128), 0), iota((128, 128), 1)
    squares = exact(spread_out, ones_where((source % NV == target % NV) & (target // NV % 2 == 0) & (target < 48)))
    turned = exact(ones_where(lane % NV == row), spread_out, ((1,), (1,)))
    fv, mixed = squares[0:NV, 0:NV], squares[NV:32, 0:NV]
    vf, mixed_t = turned[:, 0:NV], turned[:, NV:32]
    r, c = iota((NV, NV), 0), iota((NV, NV), 1)
    ff = jnp.where(c >= r, mixed, mixed_t)
    own = jnp.broadcast_to(total[4], (NV, 128))[:, 0:NV]
    vv = jnp.where(c < r, mixed, jnp.where(c > r, mixed_t, own))
    proj_ref[...] = vf
    gram = ff + exact(fv, exact(vv, vf) - 2.0 * vf)
    unit = ones_where(row + 16 == lane)
    a = jnp.pad(gram, ((0, 0), (0, 112))) + unit + jnp.where(lane >= 32, squares[0:NV], 0.0)
    columns = [jnp.broadcast_to(a[:, j : j + 1], (NV, 128)) for j in range(NV)]
    copies = []
    for k in range(0, NV, 2):
        col0, col1 = columns[k : k + 2]
        if k < NV - 2:
            at0, at1 = ({j: jnp.broadcast_to(m[j : j + 1], (NV, 128)) for j in range(k, NV)} for m in (col0, col1))
            p, q, t = at0[k], at1[k], at1[k + 1]
            scale = jnp.where(row > k + 1, 1.0 / (p * t - q * q), 0.0)
            step0, step1 = (col0 * t - col1 * q) * scale, (col1 * p - col0 * q) * scale
            row0, row1 = (jnp.broadcast_to(a[k + j : k + j + 1], (NV, 128)) for j in (0, 1))
            for j in range(k + 2, NV):
                columns[j] = columns[j] - step0 * at0[j] - step1 * at1[j]
            a = a - step0 * row0 - step1 * row1
    high, low = rows_done(a, r_ref)
    for x in range(NX):
        got = spread(xf_ref, xe_ref, xv_ref, high, low, x)
        for h in range(2):
            stage[:, x, 8 * h : 8 * h + 8, :] = got[:, NZ * h : NZ * h + NZ].reshape(NV, 8, NZ)
        if x % 1 == 1-1:
            at = (slice(None), pl.ds(x - 1 + 1, 1))
            copies.append(pltpu.make_async_copy(stage.at[at], new_ref.at[at], sems.at[x // 1]))
            copies[-1].start()
    for copy in copies:
        copy.wait()


def rows_done(a, r_ref):
    row, lane = iota((NV, 128), 0), iota((NV, 128), 1)
    above = pltpu.roll(a, 1, 0)
    before, pivot = (jnp.sum(jnp.where(lane == row - 1, m, 0.0), axis=1, keepdims=True) for m in (a, above))
    odd = row % 2 == 1
    a = a - jnp.where(odd, before / jnp.where(odd[:, 0:1], pivot, 1.0), 0.0) * above
    pivots = jnp.sum(jnp.where(row == lane, a, 0.0), axis=1, keepdims=True)
    a = a / jnp.sqrt(pivots)
    r_ref[...] = jnp.where(lane >= row, a, 0.0)[:, 0:NV]
    w = jnp.where(lane < 32, a, -a)
    w = jnp.broadcast_to(w[:, None, :], (NV, 8, 128)).reshape(128, 128)
    source, target = iota((128, 256), 0), iota((128, 256), 1)
    widen = jnp.where(source - 16 == target // 8, 1.0, 0.0).astype(BF16)
    keep = iota((128, 256), 0) % 8 == iota((128, 256), 1) % 8
    return [
        jnp.where(keep, jnp.dot(part, widen, preferred_element_type=F32), 0.0).astype(BF16) for part in two_parts(w)
    ]


def spread(xf_ref, xe_ref, xv_ref, high, low, x):
    if x in (0, NX - 1):
        f_ref, at = xe_ref, x // (NX - 1)
    else:
        f_ref, at = xf_ref, x - 1
    f_cols, v_cols = slice(256 * at, 256 * at + 256), slice(256 * x, 256 * x + 256)
    fh, fl = f_ref[0:128, f_cols], f_ref[128:256, f_cols]
    vh, vl = xv_ref[0:128, v_cols], xv_ref[128:256, v_cols]
    left = jnp.concatenate([high, high, low], axis=1)
    return jnp.dot(left, jnp.concatenate([fh, vh, fl, vl, fh, vh], axis=0), preferred_element_type=F32)


def finish(parts, xf, xe, xv):
    return pl.pallas_call(
        finish_kernel,
        out_shape=(
            jax.ShapeDtypeStruct((NV, NX, NY, NZ), F32),
            jax.ShapeDtypeStruct((NV, NV), F32),
            jax.ShapeDtypeStruct((NV, NV), F32),
        ),
        in_specs=[VMEM] * 4,
        out_specs=(pl.BlockSpec(memory_space=pl.ANY), VMEM, VMEM),
        scratch_shapes=[pltpu.VMEM((NV, NX, NY, NZ), F32), pltpu.SemaphoreType.DMA((NX,))],
        compiler_params=pltpu.CompilerParams(vmem_limit_bytes=16 << 20),
        cost_estimate=pl.CostEstimate(flops=1 << 29, bytes_accessed=3 << 20, transcendentals=0),
        name="finish",
    )(parts, xf, xe, xv)


def sent_to_all(x, axes):
    peers = lax.axis_size(axes)
    return lax.all_to_all(jnp.broadcast_to(x[None], (peers, *x.shape)), axes, 0, 0, tiled=True)


def shards(krylov_basis_block, companion, region, inv_density, stiffness, damping):
    core = lax.axis_index("slab_3").astype(jnp.int32).reshape(1)
    count = lax.axis_size(SLAB)
    *own, fields = pack(core, inv_density, stiffness, damping, krylov_basis_block, region, companion)
    pairs = [(i, i ^ 1) for i in range(count)]
    across = [(i, i + 1 if i % 2 else i - 1) for i in range(1, count - 1)]
    got0 = lax.ppermute(own[0], SLAB, across)
    got1 = lax.ppermute(own[1], SLAB, pairs)
    xf, xv, edges, tiles = main(krylov_basis_block, fields, companion)
    xe, packed, xf = edge(core, edges, tiles, xv, own, (got0, got1), xf)
    near = sent_to_all(packed.reshape(1, 640), ("slab_1", "slab_2")).sum(axis=0)
    far = sent_to_all(near.reshape(1, 640), ("slab_0", "slab_3"))
    new_block, projection, rfactor = finish(far.reshape(-1, 128), xf, xe, xv)
    return new_block, projection, rfactor


def solution(mesh):
    torus = Mesh(mesh.devices.reshape(8, 4, 8, 2), SLAB)
    placed = (
        P(None, SLAB, None, None),
        P(None, SLAB, None, None),
        P(SLAB, None, None),
        P(),
        P(),
        P(),
    )
    return jax.shard_map(
        shards,
        mesh=torus,
        in_specs=placed,
        out_specs=(P(None, SLAB, None, None), P(), P()),
        check_vma=False,
    )
```

```python
import functools

import jax
import jax.numpy as jnp
from jax import lax
from jax.experimental import pallas as pl
from jax.experimental.pallas import tpu as pltpu
from jax.sharding import Mesh
from jax.sharding import PartitionSpec as P

SLAB = ("slab_0", "slab_1", "slab_2", "slab_3")
NV, NX, NY, NZ, NR = 16, 8, 16, 128, 8
CELLS = 4096 * 16 * 128
F32, BF16 = jnp.float32, jnp.bfloat16
SMEM = pl.BlockSpec(memory_space=pltpu.SMEM)
VMEM = pl.BlockSpec(memory_space=pltpu.VMEM)


def two_parts(x):
    high = x.astype(BF16)
    return high, (x - high.astype(F32)).astype(BF16)


HBM = pl.BlockSpec(memory_space=pltpu.HBM)


def in_hbm(*arrays):
    return [pltpu.with_memory_space_constraint(a, pltpu.HBM) for a in arrays]


def pack_kernel(core, dens_ref, stiff_ref, damp_ref, v_ref, region_ref, out0, out1, fields, tables, regions, sems):
    outs = (out0, out1)
    at = ((NX - 1) * core[0], (NX - 1) * (1 - core[0]))
    whole = pltpu.make_async_copy(region_ref, regions, sems.at[0])
    small = [
        pltpu.make_async_copy(ref, tables.at[k], sems.at[1 + k]) for k, ref in enumerate((dens_ref, stiff_ref, damp_ref))
    ]
    planes = [pltpu.make_async_copy(v_ref.at[:, at[k]], outs[k].at[pl.ds(0, NV)], sems.at[4 + k]) for k in (0, 1)]
    for copy in (whole, *small, *planes):
        copy.start()
    for copy in (*small, whole):
        copy.wait()
    for x in range(NX):
        region = regions[x]
        values = [jnp.zeros(region.shape, F32)] * 3
        for r in range(NR):
            here = region == r
            values = [jnp.where(here, tables[k, r], values[k]) for k in range(3)]
        for k in range(3):
            fields[k, x] = values[k]
    for k in (0, 1):
        outs[k][NV] = fields[0, at[k]]
    for copy in planes:
        copy.wait()


def pack(core, dens, stiff, dampt, basis, region):
    plane = jax.ShapeDtypeStruct((NV + 1, NY, NZ), F32)
    return pl.pallas_call(
        pack_kernel,
        out_shape=(plane, plane, jax.ShapeDtypeStruct((3, NX, NY, NZ), F32)),
        in_specs=[SMEM] + [HBM] * 5,
        out_specs=(VMEM,) * 3,
        scratch_shapes=[
            pltpu.SMEM((3, NR), F32),
            pltpu.VMEM((NX, NY, NZ), jnp.int32),
            pltpu.SemaphoreType.DMA((6,)),
        ],
        compiler_params=pltpu.CompilerParams(vmem_limit_bytes=4 << 20),
        cost_estimate=pl.CostEstimate(flops=1 << 18, bytes_accessed=1 << 19, transcendentals=0),
        name="pack",
    )(core, *in_hbm(dens, stiff, dampt, basis, region))


def exact(left, right, dims=((1,), (0,))):
    return lax.dot_general(left, right, (dims, ((), ())), precision=lax.Precision.HIGHEST, preferred_element_type=F32)


def iota(shape, axis):
    return lax.broadcasted_iota(jnp.int32, shape, axis)


def ones_where(condition):
    return jnp.where(condition, 1.0, 0.0).astype(F32)


def folded(full):
    rows, cols = full.shape
    kept = jnp.where(iota(full.shape, 0) % 8 == iota(full.shape, 1) % 8, full, 0.0)
    return jnp.sum(kept.reshape(rows // 8, 8, cols), axis=1)


def tiled(half):
    return exact(half, ones_where(iota((128, 128), 0) // 8 == iota((128, 128), 1) % NV))


def beside(square):
    return jnp.pad(square, ((16, 0), (128, 0)))


def times_turned(left, right):
    return lax.dot_general(left, right, (((1,), (1,)), ((), ())), preferred_element_type=F32)


def products(high, low, right_high, right_low):
    left = jnp.concatenate([high, high, low], axis=1)
    right = jnp.concatenate([right_high, right_low, right_high], axis=1)
    return times_turned(left, right)


def hold_kernel(fields, basis, companion, out):
    pass


def hold(fields, basis, companion):
    anywhere = pl.BlockSpec(memory_space=pl.ANY)
    return pl.pallas_call(
        hold_kernel,
        out_shape=jax.ShapeDtypeStruct(fields.shape, fields.dtype),
        in_specs=[anywhere, HBM, HBM],
        out_specs=anywhere,
        input_output_aliases={0: 0},
        compiler_params=pltpu.CompilerParams(vmem_limit_bytes=1 << 20),
        name="hold",
    )(fields, *in_hbm(basis, companion))


def main_kernel(v_ref, fields, comp_ref, xf_ref, xv_ref, edge_ref, tiles_ref):
    yi = lax.broadcasted_iota(jnp.int32, (NY, NZ), 0)
    zi = lax.broadcasted_iota(jnp.int32, (NY, NZ), 1)
    for x in range(NX):
        for i in range(0, NV, 2):
            v0, v1 = v_ref[i, x], v_ref[i + 1, x]
            for h in range(2):
                cols, half = slice((2 * x + h) * NZ, (2 * x + h + 1) * NZ), slice(8 * h, 8 * h + 8)
                high, low = two_parts(jnp.concatenate([v0[half], v1[half]], axis=0))
                xv_ref[8 * i : 8 * i + 16, cols] = high
                xv_ref[128 + 8 * i : 144 + 8 * i, cols] = low
    for x in (0, NX - 1, *range(1, NX - 1)):
        c = fields[0, x]
        diag = -fields[1, x]
        damp = fields[2, x]
        xs = []
        for xn in (x - 1, x + 1):
            if 0 <= xn < NX:
                b = 0.5 * (c + fields[0, xn])
                diag = diag + b
                xs.append((xn, b))
        sides = []
        for shift, axis, end, at in ((NY - 1, 0, NY - 1, yi), (1, 0, 0, yi), (NZ - 1, 1, NZ - 1, zi), (1, 1, 0, zi)):
            outside = at == end
            b = jnp.where(outside, c, 0.5 * (c + pltpu.roll(c, shift, axis)))
            diag = diag + b
            sides.append((shift, axis, jnp.where(outside, 0.0, b)))

        def one(i, x=x, diag=diag, damp=damp, xs=xs, sides=sides):
            v = v_ref[i, x]
            f = diag * v + damp * comp_ref[i, x]
            for xn, b in xs:
                f = f - b * v_ref[i, xn]
            for shift, axis, b in sides:
                f = f - b * pltpu.roll(v, shift, axis)
            return f

        if x in (0, NX - 1):
            for i in range(NV):
                edge_ref[x // (NX - 1), i] = one(i)
            continue
        for i in range(0, NV, 2):
            f0, f1 = one(i), one(i + 1)
            for h in range(2):
                at = 2 * (x - 1) + h
                cols, half = slice(at * NZ, (at + 1) * NZ), slice(8 * h, 8 * h + 8)
                high, low = two_parts(jnp.concatenate([f0[half], f1[half]], axis=0))
                xf_ref[8 * i : 8 * i + 16, cols] = high
                xf_ref[128 + 8 * i : 144 + 8 * i, cols] = low
    inner, ends = slice(2 * NZ, 14 * NZ), (slice(0, 2 * NZ), slice(14 * NZ, 16 * NZ))
    high, low = (jnp.concatenate([xf_ref[k : k + 128], xv_ref[k : k + 128, inner]], axis=0) for k in (0, 128))
    end_high, end_low = (jnp.concatenate([xv_ref[k : k + 128, e] for e in ends], axis=1) for k in (0, 128))
    same, mixed = (
        folded(times_turned(high, right)) + beside(folded(times_turned(end_high, end_right)))
        for right, end_right in ((high, end_high), (low, end_low))
    )
    both = same + mixed
    square = exact(mixed, ones_where(iota((256, 128), 0) // 8 == iota((256, 128), 1)))
    group, lane = iota((32, 128), 0), iota((32, 128), 1)
    over_f, over_v = (
        tiled(both[:, 128 * k : 128 * k + 128])
        + exact(square, ones_where(group - NV * k == lane % NV), ((0,), (0,)))[0:32]
        for k in (0, 1)
    )
    tiles_ref[0:NV] = over_f[0:NV]
    tiles_ref[NV : NV + 32] = over_v


def main(basis, fields, companion):
    return pl.pallas_call(
        main_kernel,
        out_shape=(
            jax.ShapeDtypeStruct((256, 1536), BF16),
            jax.ShapeDtypeStruct((256, 2048), BF16),
            jax.ShapeDtypeStruct((2, NV, NY, NZ), F32),
            jax.ShapeDtypeStruct((48, 128), F32),
        ),
        in_specs=[VMEM] * 3,
        out_specs=(VMEM,) * 4,
        compiler_params=pltpu.CompilerParams(vmem_limit_bytes=16 << 20),
        cost_estimate=pl.CostEstimate(flops=1 << 28, bytes_accessed=5 << 20, transcendentals=0),
        name="main",
    )(basis, fields, companion)


def edge_kernel(core, edge_ref, tiles_ref, xv_ref, own0, own1, got0, got1, xf_ref, xe_ref, out_ref, kept_ref):
    upper = (core[0], 1 - core[0])
    for side, (own, got) in enumerate(((own0, got0), (own1, got1))):
        place = upper[side]
        c, other = own[NV], got[NV]
        b = 0.5 * (c + jnp.where(other > 0.0, other, c))
        for i in range(0, NV, 2):
            f0, f1 = (edge_ref[place, k] + b * (own[k] - got[k]) for k in (i, i + 1))
            for h in range(2):
                cols, half = pl.ds(pl.multiple_of((place * 2 + h) * NZ, NZ), NZ), slice(8 * h, 8 * h + 8)
                high, low = two_parts(jnp.concatenate([f0[half], f1[half]], axis=0))
                xe_ref[8 * i : 8 * i + 16, cols] = high
                xe_ref[128 + 8 * i : 144 + 8 * i, cols] = low
    fh, fl = xe_ref[0:128], xe_ref[128:256]
    ends = (slice(0, 2 * NZ), slice(14 * NZ, 16 * NZ))
    vh, vl = (jnp.concatenate([xv_ref[k : k + 128, e] for e in ends], axis=1) for k in (0, 128))
    sums = folded(products(fh, fl, jnp.concatenate([fh, vh], axis=0), jnp.concatenate([fl, vl], axis=0)))
    over = tiled(jnp.concatenate([sums[:, 0:128], sums[:, 128:256]], axis=0)) + tiles_ref[0:32]
    ff, fv = over[0:NV], over[NV:32]
    vv = tiles_ref[32:48]
    row, lane = iota((NV, 128), 0), iota((NV, 128), 1)
    sums = []
    for m in (fv, jnp.where(lane % NV >= row, ff, vv)):
        m = jnp.where(lane // NV == row % 8, m, 0.0)
        sums += [jnp.sum(m[0:8], axis=0, keepdims=True), jnp.sum(m[8:16], axis=0, keepdims=True)]
    sums.append(jnp.sum(jnp.where(lane == row, vv, 0.0), axis=0, keepdims=True))
    for k, m in enumerate(sums):
        out_ref[k : k + 1] = m * (1.0 / CELLS)


def edge(core, edges, tiles, xv, own, got, xf):
    anywhere = pl.BlockSpec(memory_space=pl.ANY)
    return pl.pallas_call(
        edge_kernel,
        out_shape=(
            jax.ShapeDtypeStruct((256, 512), BF16),
            jax.ShapeDtypeStruct((5, 128), F32),
            jax.ShapeDtypeStruct(xf.shape, xf.dtype),
        ),
        in_specs=[SMEM] + [VMEM] * 7 + [anywhere],
        out_specs=(VMEM, VMEM, anywhere),
        input_output_aliases={8: 2},
        compiler_params=pltpu.CompilerParams(vmem_limit_bytes=8 << 20),
        cost_estimate=pl.CostEstimate(flops=1 << 27, bytes_accessed=2 << 20, transcendentals=0),
        name="edge",
    )(core, edges, tiles, xv, *own, *got, xf)


def summed(left, right):
    terms = [left[:, k : k + 1] * right[k : k + 1] for k in range(NV)]
    while len(terms) > 1:
        terms = [a + b for a, b in zip(terms[::2], terms[1::2])]
    return terms[0]


def finish_kernel(parts_ref, xf_ref, xe_ref, xv_ref, new_ref, proj_ref, r_ref, stage, sems):
    row, lane = iota((NV, 128), 0), iota((NV, 128), 1)
    total = [jnp.sum(parts_ref[pl.ds(k, parts_ref.shape[0] // 5, stride=5), :], axis=0, keepdims=True) for k in range(5)]
    mine = lane // NV == row % 8
    spread_out = [
        jnp.where(mine, jnp.where(row < 8, jnp.broadcast_to(lo, (NV, 128)), jnp.broadcast_to(hi, (NV, 128))), 0.0)
        for lo, hi in ((total[0], total[1]), (total[2], total[3]))
    ]
    spread_out = jnp.concatenate(spread_out, axis=0)
    source, target = iota((128, 128), 0), iota((128, 128), 1)
    squares = exact(spread_out, ones_where((source % NV == target % NV) & (target // NV % 2 == 0) & (target < 48)))
    turned = exact(ones_where(lane % NV == row), spread_out, ((1,), (1,)))
    fv, mixed = squares[0:NV, 0:NV], squares[NV:32, 0:NV]
    vf, mixed_t = turned[:, 0:NV], turned[:, NV:32]
    r, c = iota((NV, NV), 0), iota((NV, NV), 1)
    ff = jnp.where(c >= r, mixed, mixed_t)
    own = jnp.broadcast_to(total[4], (NV, 128))[:, 0:NV]
    vv = jnp.where(c < r, mixed, jnp.where(c > r, mixed_t, own))
    proj_ref[...] = vf
    gram = ff + summed(fv, summed(vv, vf) - 2.0 * vf)
    unit = ones_where(row + 16 == lane)
    a = jnp.pad(gram, ((0, 0), (0, 112))) + unit + jnp.where(lane >= 32, squares[0:NV], 0.0)
    columns = [jnp.broadcast_to(a[:, j : j + 1], (NV, 128)) for j in range(NV)]
    copies = []
    for k in range(0, NV, 2):
        col0, col1 = columns[k : k + 2]
        if k < NV - 2:
            at0, at1 = ({j: jnp.broadcast_to(m[j : j + 1], (NV, 128)) for j in range(k, NV)} for m in (col0, col1))
            p, q, t = at0[k], at1[k], at1[k + 1]
            scale = jnp.where(row > k + 1, 1.0 / (p * t - q * q), 0.0)
            step0, step1 = (col0 * t - col1 * q) * scale, (col1 * p - col0 * q) * scale
            row0, row1 = (jnp.broadcast_to(a[k + j : k + j + 1], (NV, 128)) for j in (0, 1))
            for j in range(k + 2, NV):
                columns[j] = columns[j] - step0 * at0[j] - step1 * at1[j]
            a = a - step0 * row0 - step1 * row1
    high, low = rows_done(a, r_ref)
    for x in range(NX):
        got = spread(xf_ref, xe_ref, xv_ref, high, low, x)
        for h in range(2):
            stage[:, x, 8 * h : 8 * h + 8, :] = got[:, NZ * h : NZ * h + NZ].reshape(NV, 8, NZ)
        if x % 1 == 1-1:
            at = (slice(None), pl.ds(x - 1 + 1, 1))
            copies.append(pltpu.make_async_copy(stage.at[at], new_ref.at[at], sems.at[x // 1]))
            copies[-1].start()
    for copy in copies:
        copy.wait()


def rows_done(a, r_ref):
    row, lane = iota((NV, 128), 0), iota((NV, 128), 1)
    above = pltpu.roll(a, 1, 0)
    before, pivot = (jnp.sum(jnp.where(lane == row - 1, m, 0.0), axis=1, keepdims=True) for m in (a, above))
    odd = row % 2 == 1
    a = a - jnp.where(odd, before / jnp.where(odd[:, 0:1], pivot, 1.0), 0.0) * above
    pivots = jnp.sum(jnp.where(row == lane, a, 0.0), axis=1, keepdims=True)
    a = a / jnp.sqrt(pivots)
    r_ref[...] = jnp.where(lane >= row, a, 0.0)[:, 0:NV]
    w = jnp.where(lane < 32, a, -a)
    w = jnp.broadcast_to(w[:, None, :], (NV, 8, 128)).reshape(128, 128)
    source, target = iota((128, 256), 0), iota((128, 256), 1)
    widen = jnp.where(source - 16 == target // 8, 1.0, 0.0).astype(BF16)
    keep = iota((128, 256), 0) % 8 == iota((128, 256), 1) % 8
    return [
        jnp.where(keep, jnp.dot(part, widen, preferred_element_type=F32), 0.0).astype(BF16) for part in two_parts(w)
    ]


def spread(xf_ref, xe_ref, xv_ref, high, low, x):
    if x in (0, NX - 1):
        f_ref, at = xe_ref, x // (NX - 1)
    else:
        f_ref, at = xf_ref, x - 1
    f_cols, v_cols = slice(256 * at, 256 * at + 256), slice(256 * x, 256 * x + 256)
    fh, fl = f_ref[0:128, f_cols], f_ref[128:256, f_cols]
    vh, vl = xv_ref[0:128, v_cols], xv_ref[128:256, v_cols]
    left = jnp.concatenate([high, high, low], axis=1)
    return jnp.dot(left, jnp.concatenate([fh, vh, fl, vl, fh, vh], axis=0), preferred_element_type=F32)


def finish(parts, xf, xe, xv):
    return pl.pallas_call(
        finish_kernel,
        out_shape=(
            jax.ShapeDtypeStruct((NV, NX, NY, NZ), F32),
            jax.ShapeDtypeStruct((NV, NV), F32),
            jax.ShapeDtypeStruct((NV, NV), F32),
        ),
        in_specs=[VMEM] * 4,
        out_specs=(pl.BlockSpec(memory_space=pl.ANY), VMEM, VMEM),
        scratch_shapes=[pltpu.VMEM((NV, NX, NY, NZ), F32), pltpu.SemaphoreType.DMA((NX,))],
        compiler_params=pltpu.CompilerParams(vmem_limit_bytes=16 << 20),
        cost_estimate=pl.CostEstimate(flops=1 << 29, bytes_accessed=3 << 20, transcendentals=0),
        name="finish",
    )(parts, xf, xe, xv)


def sent_to_all(x, axes):
    peers = lax.axis_size(axes)
    return lax.all_to_all(jnp.broadcast_to(x[None], (peers, *x.shape)), axes, 0, 0, tiled=True)


def shards(krylov_basis_block, companion, region, inv_density, stiffness, damping):
    core = lax.axis_index("slab_3").astype(jnp.int32).reshape(1)
    count = lax.axis_size(SLAB)
    *own, fields = pack(core, inv_density, stiffness, damping, krylov_basis_block, region)
    own[0] = hold(own[0], krylov_basis_block, companion)
    pairs = [(i, i ^ 1) for i in range(count)]
    across = [(i, i + 1 if i % 2 else i - 1) for i in range(1, count - 1)]
    got0 = lax.ppermute(own[0], SLAB, across)
    got1 = lax.ppermute(own[1], SLAB, pairs)
    xf, xv, edges, tiles = main(krylov_basis_block, fields, companion)
    xe, packed, xf = edge(core, edges, tiles, xv, own, (got0, got1), xf)
    near = sent_to_all(packed.reshape(1, 640), ("slab_1", "slab_2")).sum(axis=0)
    far = sent_to_all(near.reshape(1, 640), ("slab_0", "slab_3"))
    new_block, projection, rfactor = finish(far.reshape(-1, 128), xf, xe, xv)
    return new_block, projection, rfactor


def solution(mesh):
    torus = Mesh(mesh.devices.reshape(8, 4, 8, 2), SLAB)
    placed = (
        P(None, SLAB, None, None),
        P(None, SLAB, None, None),
        P(SLAB, None, None),
        P(),
        P(),
        P(),
    )
    return jax.shard_map(
        shards,
        mesh=torus,
        in_specs=placed,
        out_specs=(P(None, SLAB, None, None), P(), P()),
        check_vma=False,
    )
```

```python
import functools

import jax
import jax.numpy as jnp
from jax import lax
from jax.experimental import pallas as pl
from jax.experimental.pallas import tpu as pltpu
from jax.sharding import Mesh
from jax.sharding import PartitionSpec as P

SLAB = ("slab_0", "slab_1", "slab_2", "slab_3")
NV, NX, NY, NZ, NR = 16, 8, 16, 128, 8
CELLS = 4096 * 16 * 128
F32, BF16 = jnp.float32, jnp.bfloat16
SMEM = pl.BlockSpec(memory_space=pltpu.SMEM)
VMEM = pl.BlockSpec(memory_space=pltpu.VMEM)


def two_parts(x):
    high = x.astype(BF16)
    return high, (x - high.astype(F32)).astype(BF16)


HBM = pl.BlockSpec(memory_space=pltpu.HBM)


def in_hbm(*arrays):
    return [pltpu.with_memory_space_constraint(a, pltpu.HBM) for a in arrays]


def pack_kernel(core, dens_ref, stiff_ref, damp_ref, v_ref, region_ref, out0, out1, fields, tables, regions, sems):
    outs = (out0, out1)
    at = ((NX - 1) * core[0], (NX - 1) * (1 - core[0]))
    whole = pltpu.make_async_copy(region_ref, regions, sems.at[0])
    small = [
        pltpu.make_async_copy(ref, tables.at[k], sems.at[1 + k]) for k, ref in enumerate((dens_ref, stiff_ref, damp_ref))
    ]
    planes = [pltpu.make_async_copy(v_ref.at[:, at[k]], outs[k].at[pl.ds(0, NV)], sems.at[4 + k]) for k in (0, 1)]
    for copy in (whole, *small, *planes):
        copy.start()
    for copy in (*small, whole):
        copy.wait()
    for x in range(NX):
        region = regions[x]
        values = [jnp.zeros(region.shape, F32)] * 3
        for r in range(NR):
            here = region == r
            values = [jnp.where(here, tables[k, r], values[k]) for k in range(3)]
        for k in range(3):
            fields[k, x] = values[k]
    for k in (0, 1):
        outs[k][NV] = fields[0, at[k]]
    for copy in planes:
        copy.wait()


def pack(core, dens, stiff, dampt, basis, region):
    plane = jax.ShapeDtypeStruct((NV + 1, NY, NZ), F32)
    return pl.pallas_call(
        pack_kernel,
        out_shape=(plane, plane, jax.ShapeDtypeStruct((3, NX, NY, NZ), F32)),
        in_specs=[SMEM] + [HBM] * 5,
        out_specs=(VMEM,) * 3,
        scratch_shapes=[
            pltpu.SMEM((3, NR), F32),
            pltpu.VMEM((NX, NY, NZ), jnp.int32),
            pltpu.SemaphoreType.DMA((6,)),
        ],
        compiler_params=pltpu.CompilerParams(vmem_limit_bytes=4 << 20),
        cost_estimate=pl.CostEstimate(flops=1 << 18, bytes_accessed=1 << 19, transcendentals=0),
        name="pack",
    )(core, *in_hbm(dens, stiff, dampt, basis, region))


def iota(shape, axis):
    return lax.broadcasted_iota(jnp.int32, shape, axis)


def ones_where(condition):
    return jnp.where(condition, 1.0, 0.0).astype(F32)


def picked(values, chosen, dims=((1,), (0,)), values_first=True):
    first, rest = values.astype(BF16), values
    parts = [first]
    for _ in range(2):
        rest = rest - parts[-1].astype(F32)
        parts.append(rest.astype(BF16))
    ones = jnp.where(chosen, 1.0, 0.0).astype(BF16)
    values_dim, ones_dim = (dims[0][0], dims[1][0]) if values_first else (dims[1][0], dims[0][0])
    values, ones = jnp.concatenate(parts, axis=values_dim), jnp.concatenate([ones] * 3, axis=ones_dim)
    left, right = (values, ones) if values_first else (ones, values)
    return lax.dot_general(left, right, (dims, ((), ())), preferred_element_type=F32)


def folded(full):
    rows, cols = full.shape
    kept = jnp.where(iota(full.shape, 0) % 8 == iota(full.shape, 1) % 8, full, 0.0)
    return jnp.sum(kept.reshape(rows // 8, 8, cols), axis=1)


def tiled(half):
    return picked(half, iota((128, 128), 0) // 8 == iota((128, 128), 1) % NV)


def beside(square):
    return jnp.pad(square, ((16, 0), (128, 0)))


def times_turned(left, right):
    return lax.dot_general(left, right, (((1,), (1,)), ((), ())), preferred_element_type=F32)


def products(high, low, right_high, right_low):
    left = jnp.concatenate([high, high, low], axis=1)
    right = jnp.concatenate([right_high, right_low, right_high], axis=1)
    return times_turned(left, right)


def hold_kernel(fields, basis, companion, out):
    pass


def hold(fields, basis, companion):
    anywhere = pl.BlockSpec(memory_space=pl.ANY)
    return pl.pallas_call(
        hold_kernel,
        out_shape=jax.ShapeDtypeStruct(fields.shape, fields.dtype),
        in_specs=[anywhere, HBM, HBM],
        out_specs=anywhere,
        input_output_aliases={0: 0},
        compiler_params=pltpu.CompilerParams(vmem_limit_bytes=1 << 20),
        name="hold",
    )(fields, *in_hbm(basis, companion))


def main_kernel(v_ref, fields, comp_ref, xf_ref, xv_ref, edge_ref, tiles_ref):
    yi = lax.broadcasted_iota(jnp.int32, (NY, NZ), 0)
    zi = lax.broadcasted_iota(jnp.int32, (NY, NZ), 1)
    for x in range(NX):
        for i in range(0, NV, 2):
            v0, v1 = v_ref[i, x], v_ref[i + 1, x]
            for h in range(2):
                cols, half = slice((2 * x + h) * NZ, (2 * x + h + 1) * NZ), slice(8 * h, 8 * h + 8)
                high, low = two_parts(jnp.concatenate([v0[half], v1[half]], axis=0))
                xv_ref[8 * i : 8 * i + 16, cols] = high
                xv_ref[128 + 8 * i : 144 + 8 * i, cols] = low
    for x in (0, NX - 1, *range(1, NX - 1)):
        c = fields[0, x]
        diag = -fields[1, x]
        damp = fields[2, x]
        xs = []
        for xn in (x - 1, x + 1):
            if 0 <= xn < NX:
                b = 0.5 * (c + fields[0, xn])
                diag = diag + b
                xs.append((xn, b))
        sides = []
        for shift, axis, end, at in ((NY - 1, 0, NY - 1, yi), (1, 0, 0, yi), (NZ - 1, 1, NZ - 1, zi), (1, 1, 0, zi)):
            outside = at == end
            b = jnp.where(outside, c, 0.5 * (c + pltpu.roll(c, shift, axis)))
            diag = diag + b
            sides.append((shift, axis, jnp.where(outside, 0.0, b)))

        def one(i, x=x, diag=diag, damp=damp, xs=xs, sides=sides):
            v = v_ref[i, x]
            f = diag * v + damp * comp_ref[i, x]
            for xn, b in xs:
                f = f - b * v_ref[i, xn]
            for shift, axis, b in sides:
                f = f - b * pltpu.roll(v, shift, axis)
            return f

        if x in (0, NX - 1):
            for i in range(NV):
                edge_ref[x // (NX - 1), i] = one(i)
            continue
        for i in range(0, NV, 2):
            f0, f1 = one(i), one(i + 1)
            for h in range(2):
                at = 2 * (x - 1) + h
                cols, half = slice(at * NZ, (at + 1) * NZ), slice(8 * h, 8 * h + 8)
                high, low = two_parts(jnp.concatenate([f0[half], f1[half]], axis=0))
                xf_ref[8 * i : 8 * i + 16, cols] = high
                xf_ref[128 + 8 * i : 144 + 8 * i, cols] = low
    inner, ends = slice(2 * NZ, 14 * NZ), (slice(0, 2 * NZ), slice(14 * NZ, 16 * NZ))
    high, low = (jnp.concatenate([xf_ref[k : k + 128], xv_ref[k : k + 128, inner]], axis=0) for k in (0, 128))
    end_high, end_low = (jnp.concatenate([xv_ref[k : k + 128, e] for e in ends], axis=1) for k in (0, 128))
    same, mixed = (
        folded(times_turned(high, right)) + beside(folded(times_turned(end_high, end_right)))
        for right, end_right in ((high, end_high), (low, end_low))
    )
    both = same + mixed
    group, lane = iota((32, 128), 0), iota((32, 128), 1)
    over_f, over_v = (
        tiled(both[:, 128 * k : 128 * k + 128])
        + jnp.sum(picked(mixed, group - NV * k == lane % NV, ((0,), (0,))).reshape(32, 8, 128), axis=1)
        for k in (0, 1)
    )
    tiles_ref[0:NV] = over_f[0:NV]
    tiles_ref[NV : NV + 32] = over_v


def main(basis, fields, companion):
    return pl.pallas_call(
        main_kernel,
        out_shape=(
            jax.ShapeDtypeStruct((256, 1536), BF16),
            jax.ShapeDtypeStruct((256, 2048), BF16),
            jax.ShapeDtypeStruct((2, NV, NY, NZ), F32),
            jax.ShapeDtypeStruct((48, 128), F32),
        ),
        in_specs=[VMEM] * 3,
        out_specs=(VMEM,) * 4,
        compiler_params=pltpu.CompilerParams(vmem_limit_bytes=16 << 20),
        cost_estimate=pl.CostEstimate(flops=1 << 28, bytes_accessed=5 << 20, transcendentals=0),
        name="main",
    )(basis, fields, companion)


def edge_kernel(core, edge_ref, tiles_ref, xv_ref, own0, own1, got0, got1, xf_ref, xe_ref, out_ref, kept_ref):
    upper = (core[0], 1 - core[0])
    for side, (own, got) in enumerate(((own0, got0), (own1, got1))):
        place = upper[side]
        c, other = own[NV], got[NV]
        b = 0.5 * (c + jnp.where(other > 0.0, other, c))
        for i in range(0, NV, 2):
            f0, f1 = (edge_ref[place, k] + b * (own[k] - got[k]) for k in (i, i + 1))
            for h in range(2):
                cols, half = pl.ds(pl.multiple_of((place * 2 + h) * NZ, NZ), NZ), slice(8 * h, 8 * h + 8)
                high, low = two_parts(jnp.concatenate([f0[half], f1[half]], axis=0))
                xe_ref[8 * i : 8 * i + 16, cols] = high
                xe_ref[128 + 8 * i : 144 + 8 * i, cols] = low
    fh, fl = xe_ref[0:128], xe_ref[128:256]
    ends = (slice(0, 2 * NZ), slice(14 * NZ, 16 * NZ))
    vh, vl = (jnp.concatenate([xv_ref[k : k + 128, e] for e in ends], axis=1) for k in (0, 128))
    sums = folded(products(fh, fl, jnp.concatenate([fh, vh], axis=0), jnp.concatenate([fl, vl], axis=0)))
    over = tiled(jnp.concatenate([sums[:, 0:128], sums[:, 128:256]], axis=0)) + tiles_ref[0:32]
    ff, fv = over[0:NV], over[NV:32]
    vv = tiles_ref[32:48]
    row, lane = iota((NV, 128), 0), iota((NV, 128), 1)
    sums = []
    for m in (fv, jnp.where(lane % NV >= row, ff, vv)):
        m = jnp.where(lane // NV == row % 8, m, 0.0)
        sums += [jnp.sum(m[0:8], axis=0, keepdims=True), jnp.sum(m[8:16], axis=0, keepdims=True)]
    sums.append(jnp.sum(jnp.where(lane == row, vv, 0.0), axis=0, keepdims=True))
    for k, m in enumerate(sums):
        out_ref[k : k + 1] = m * (1.0 / CELLS)


def edge(core, edges, tiles, xv, own, got, xf):
    anywhere = pl.BlockSpec(memory_space=pl.ANY)
    return pl.pallas_call(
        edge_kernel,
        out_shape=(
            jax.ShapeDtypeStruct((256, 512), BF16),
            jax.ShapeDtypeStruct((5, 128), F32),
            jax.ShapeDtypeStruct(xf.shape, xf.dtype),
        ),
        in_specs=[SMEM] + [VMEM] * 7 + [anywhere],
        out_specs=(VMEM, VMEM, anywhere),
        input_output_aliases={8: 2},
        compiler_params=pltpu.CompilerParams(vmem_limit_bytes=8 << 20),
        cost_estimate=pl.CostEstimate(flops=1 << 27, bytes_accessed=2 << 20, transcendentals=0),
        name="edge",
    )(core, edges, tiles, xv, *own, *got, xf)


def summed(left, right):
    terms = [left[:, k : k + 1] * right[k : k + 1] for k in range(NV)]
    while len(terms) > 1:
        terms = [a + b for a, b in zip(terms[::2], terms[1::2])]
    return terms[0]


def finish_kernel(parts_ref, xf_ref, xe_ref, xv_ref, new_ref, proj_ref, r_ref, stage, sems):
    row, lane = iota((NV, 128), 0), iota((NV, 128), 1)
    total = [jnp.sum(parts_ref[pl.ds(k, parts_ref.shape[0] // 5, stride=5), :], axis=0, keepdims=True) for k in range(5)]
    mine = lane // NV == row % 8
    spread_out = [
        jnp.where(mine, jnp.where(row < 8, jnp.broadcast_to(lo, (NV, 128)), jnp.broadcast_to(hi, (NV, 128))), 0.0)
        for lo, hi in ((total[0], total[1]), (total[2], total[3]))
    ]
    spread_out = jnp.concatenate(spread_out, axis=0)
    source, target = iota((128, 128), 0), iota((128, 128), 1)
    squares = picked(spread_out, (source % NV == target % NV) & (target // NV % 2 == 0) & (target < 48))
    turned = picked(spread_out, lane % NV == row, ((1,), (1,)), values_first=False)
    fv, mixed = squares[0:NV, 0:NV], squares[NV:32, 0:NV]
    vf, mixed_t = turned[:, 0:NV], turned[:, NV:32]
    r, c = iota((NV, NV), 0), iota((NV, NV), 1)
    ff = jnp.where(c >= r, mixed, mixed_t)
    own = jnp.broadcast_to(total[4], (NV, 128))[:, 0:NV]
    vv = jnp.where(c < r, mixed, jnp.where(c > r, mixed_t, own))
    proj_ref[...] = vf
    gram = ff + summed(fv, summed(vv, vf) - 2.0 * vf)
    unit = ones_where(row + 16 == lane)
    a = jnp.pad(gram, ((0, 0), (0, 112))) + unit + jnp.where(lane >= 32, squares[0:NV], 0.0)
    columns = [jnp.broadcast_to(a[:, j : j + 1], (NV, 128)) for j in range(NV)]
    copies = []
    for k in range(0, NV, 2):
        col0, col1 = columns[k : k + 2]
        if k < NV - 2:
            at0, at1 = ({j: jnp.broadcast_to(m[j : j + 1], (NV, 128)) for j in range(k, NV)} for m in (col0, col1))
            p, q, t = at0[k], at1[k], at1[k + 1]
            scale = jnp.where(row > k + 1, 1.0 / (p * t - q * q), 0.0)
            step0, step1 = (col0 * t - col1 * q) * scale, (col1 * p - col0 * q) * scale
            row0, row1 = (jnp.broadcast_to(a[k + j : k + j + 1], (NV, 128)) for j in (0, 1))
            for j in range(k + 2, NV):
                columns[j] = columns[j] - step0 * at0[j] - step1 * at1[j]
            a = a - step0 * row0 - step1 * row1
    high, low = rows_done(a, r_ref)
    for x in range(NX):
        got = spread(xf_ref, xe_ref, xv_ref, high, low, x)
        for h in range(2):
            stage[:, x, 8 * h : 8 * h + 8, :] = got[:, NZ * h : NZ * h + NZ].reshape(NV, 8, NZ)
        if x % 1 == 1-1:
            at = (slice(None), pl.ds(x - 1 + 1, 1))
            copies.append(pltpu.make_async_copy(stage.at[at], new_ref.at[at], sems.at[x // 1]))
            copies[-1].start()
    for copy in copies:
        copy.wait()


def rows_done(a, r_ref):
    row, lane = iota((NV, 128), 0), iota((NV, 128), 1)
    above = pltpu.roll(a, 1, 0)
    before, pivot = (jnp.sum(jnp.where(lane == row - 1, m, 0.0), axis=1, keepdims=True) for m in (a, above))
    odd = row % 2 == 1
    a = a - jnp.where(odd, before / jnp.where(odd[:, 0:1], pivot, 1.0), 0.0) * above
    pivots = jnp.sum(jnp.where(row == lane, a, 0.0), axis=1, keepdims=True)
    a = a / jnp.sqrt(pivots)
    r_ref[...] = jnp.where(lane >= row, a, 0.0)[:, 0:NV]
    w = jnp.where(lane < 32, a, -a)
    w = jnp.broadcast_to(w[:, None, :], (NV, 8, 128)).reshape(128, 128)
    source, target = iota((128, 256), 0), iota((128, 256), 1)
    widen = jnp.where(source - 16 == target // 8, 1.0, 0.0).astype(BF16)
    keep = iota((128, 256), 0) % 8 == iota((128, 256), 1) % 8
    return [
        jnp.where(keep, jnp.dot(part, widen, preferred_element_type=F32), 0.0).astype(BF16) for part in two_parts(w)
    ]


def spread(xf_ref, xe_ref, xv_ref, high, low, x):
    if x in (0, NX - 1):
        f_ref, at = xe_ref, x // (NX - 1)
    else:
        f_ref, at = xf_ref, x - 1
    f_cols, v_cols = slice(256 * at, 256 * at + 256), slice(256 * x, 256 * x + 256)
    fh, fl = f_ref[0:128, f_cols], f_ref[128:256, f_cols]
    vh, vl = xv_ref[0:128, v_cols], xv_ref[128:256, v_cols]
    left = jnp.concatenate([high, high, low], axis=1)
    return jnp.dot(left, jnp.concatenate([fh, vh, fl, vl, fh, vh], axis=0), preferred_element_type=F32)


def finish(parts, xf, xe, xv):
    return pl.pallas_call(
        finish_kernel,
        out_shape=(
            jax.ShapeDtypeStruct((NV, NX, NY, NZ), F32),
            jax.ShapeDtypeStruct((NV, NV), F32),
            jax.ShapeDtypeStruct((NV, NV), F32),
        ),
        in_specs=[VMEM] * 4,
        out_specs=(pl.BlockSpec(memory_space=pl.ANY), VMEM, VMEM),
        scratch_shapes=[pltpu.VMEM((NV, NX, NY, NZ), F32), pltpu.SemaphoreType.DMA((NX,))],
        compiler_params=pltpu.CompilerParams(vmem_limit_bytes=16 << 20),
        cost_estimate=pl.CostEstimate(flops=1 << 29, bytes_accessed=3 << 20, transcendentals=0),
        name="finish",
    )(parts, xf, xe, xv)


def sent_to_all(x, axes):
    peers = lax.axis_size(axes)
    return lax.all_to_all(jnp.broadcast_to(x[None], (peers, *x.shape)), axes, 0, 0, tiled=True)


def shards(krylov_basis_block, companion, region, inv_density, stiffness, damping):
    core = lax.axis_index("slab_3").astype(jnp.int32).reshape(1)
    count = lax.axis_size(SLAB)
    *own, fields = pack(core, inv_density, stiffness, damping, krylov_basis_block, region)
    own[0] = hold(own[0], krylov_basis_block, companion)
    pairs = [(i, i ^ 1) for i in range(count)]
    across = [(i, i + 1 if i % 2 else i - 1) for i in range(1, count - 1)]
    got0 = lax.ppermute(own[0], SLAB, across)
    got1 = lax.ppermute(own[1], SLAB, pairs)
    xf, xv, edges, tiles = main(krylov_basis_block, fields, companion)
    xe, packed, xf = edge(core, edges, tiles, xv, own, (got0, got1), xf)
    near = sent_to_all(packed.reshape(1, 640), ("slab_1", "slab_2")).sum(axis=0)
    far = sent_to_all(near.reshape(1, 640), ("slab_0", "slab_3"))
    new_block, projection, rfactor = finish(far.reshape(-1, 128), xf, xe, xv)
    return new_block, projection, rfactor


def solution(mesh):
    torus = Mesh(mesh.devices.reshape(8, 4, 8, 2), SLAB)
    placed = (
        P(None, SLAB, None, None),
        P(None, SLAB, None, None),
        P(SLAB, None, None),
        P(),
        P(),
        P(),
    )
    return jax.shard_map(
        shards,
        mesh=torus,
        in_specs=placed,
        out_specs=(P(None, SLAB, None, None), P(), P()),
        check_vma=False,
    )
```

```python
import functools

import jax
import jax.numpy as jnp
from jax import lax
from jax.experimental import pallas as pl
from jax.experimental.pallas import tpu as pltpu
from jax.sharding import Mesh
from jax.sharding import PartitionSpec as P

SLAB = ("slab_0", "slab_1", "slab_2", "slab_3")
NV, NX, NY, NZ, NR = 16, 8, 16, 128, 8
CELLS = 4096 * 16 * 128
F32, BF16 = jnp.float32, jnp.bfloat16
SMEM = pl.BlockSpec(memory_space=pltpu.SMEM)
VMEM = pl.BlockSpec(memory_space=pltpu.VMEM)


def two_parts(x):
    high = x.astype(BF16)
    return high, (x - high.astype(F32)).astype(BF16)


HBM = pl.BlockSpec(memory_space=pltpu.HBM)


def in_hbm(*arrays):
    return [pltpu.with_memory_space_constraint(a, pltpu.HBM) for a in arrays]


def pack_kernel(core, dens_ref, stiff_ref, damp_ref, v_ref, region_ref, out0, out1, fields, tables, regions, sems):
    outs = (out0, out1)
    at = ((NX - 1) * core[0], (NX - 1) * (1 - core[0]))
    whole = pltpu.make_async_copy(region_ref, regions, sems.at[0])
    small = [
        pltpu.make_async_copy(ref, tables.at[k], sems.at[1 + k]) for k, ref in enumerate((dens_ref, stiff_ref, damp_ref))
    ]
    planes = [pltpu.make_async_copy(v_ref.at[:, at[k]], outs[k].at[pl.ds(0, NV)], sems.at[4 + k]) for k in (0, 1)]
    for copy in (whole, *small, *planes):
        copy.start()
    for copy in (*small, whole):
        copy.wait()
    for x in range(NX):
        region = regions[x]
        values = [jnp.zeros(region.shape, F32)] * 3
        for r in range(NR):
            here = region == r
            values = [jnp.where(here, tables[k, r], values[k]) for k in range(3)]
        for k in range(3):
            fields[k, x] = values[k]
    for k in (0, 1):
        outs[k][NV] = fields[0, at[k]]
    for copy in planes:
        copy.wait()


def pack(core, dens, stiff, dampt, basis, region):
    plane = jax.ShapeDtypeStruct((NV + 1, NY, NZ), F32)
    return pl.pallas_call(
        pack_kernel,
        out_shape=(plane, plane, jax.ShapeDtypeStruct((3, NX, NY, NZ), F32)),
        in_specs=[SMEM] + [HBM] * 5,
        out_specs=(VMEM,) * 3,
        scratch_shapes=[
            pltpu.SMEM((3, NR), F32),
            pltpu.VMEM((NX, NY, NZ), jnp.int32),
            pltpu.SemaphoreType.DMA((6,)),
        ],
        compiler_params=pltpu.CompilerParams(vmem_limit_bytes=4 << 20),
        cost_estimate=pl.CostEstimate(flops=1 << 18, bytes_accessed=1 << 19, transcendentals=0),
        name="pack",
    )(core, *in_hbm(dens, stiff, dampt, basis, region))


def iota(shape, axis):
    return lax.broadcasted_iota(jnp.int32, shape, axis)


def ones_where(condition):
    return jnp.where(condition, 1.0, 0.0).astype(F32)


def picked(values, chosen, dims=((1,), (0,)), values_first=True):
    first, rest = values.astype(BF16), values
    parts = [first]
    for _ in range(2):
        rest = rest - parts[-1].astype(F32)
        parts.append(rest.astype(BF16))
    ones = jnp.where(chosen, 1.0, 0.0).astype(BF16)
    values_dim, ones_dim = (dims[0][0], dims[1][0]) if values_first else (dims[1][0], dims[0][0])
    values, ones = jnp.concatenate(parts, axis=values_dim), jnp.concatenate([ones] * 3, axis=ones_dim)
    left, right = (values, ones) if values_first else (ones, values)
    return lax.dot_general(left, right, (dims, ((), ())), preferred_element_type=F32)


def folded(full):
    rows, cols = full.shape
    kept = jnp.where(iota(full.shape, 0) % 8 == iota(full.shape, 1) % 8, full, 0.0)
    return jnp.sum(kept.reshape(rows // 8, 8, cols), axis=1)


def tiled(half):
    return picked(half, iota((128, 128), 0) // 8 == iota((128, 128), 1) % NV)


def beside(square):
    return jnp.pad(square, ((16, 0), (128, 0)))


def times_turned(left, right):
    return lax.dot_general(left, right, (((1,), (1,)), ((), ())), preferred_element_type=F32)


def products(high, low, right_high, right_low):
    left = jnp.concatenate([high, high, low], axis=1)
    right = jnp.concatenate([right_high, right_low, right_high], axis=1)
    return times_turned(left, right)


def hold_kernel(fields, basis, companion, out):
    pass


def hold(fields, basis, companion):
    anywhere = pl.BlockSpec(memory_space=pl.ANY)
    return pl.pallas_call(
        hold_kernel,
        out_shape=jax.ShapeDtypeStruct(fields.shape, fields.dtype),
        in_specs=[anywhere, HBM, HBM],
        out_specs=anywhere,
        input_output_aliases={0: 0},
        compiler_params=pltpu.CompilerParams(vmem_limit_bytes=1 << 20),
        name="hold",
    )(fields, *in_hbm(basis, companion))


def main_kernel(v_ref, fields, comp_ref, xf_ref, xv_ref, edge_ref, tiles_ref):
    yi = lax.broadcasted_iota(jnp.int32, (NY, NZ), 0)
    zi = lax.broadcasted_iota(jnp.int32, (NY, NZ), 1)
    for x in range(NX):
        for i in range(0, NV, 2):
            v0, v1 = v_ref[i, x], v_ref[i + 1, x]
            for h in range(2):
                cols, half = slice((2 * x + h) * NZ, (2 * x + h + 1) * NZ), slice(8 * h, 8 * h + 8)
                high, low = two_parts(jnp.concatenate([v0[half], v1[half]], axis=0))
                xv_ref[8 * i : 8 * i + 16, cols] = high
                xv_ref[128 + 8 * i : 144 + 8 * i, cols] = low
    for x in (0, NX - 1, *range(1, NX - 1)):
        c = fields[0, x]
        diag = -fields[1, x]
        damp = fields[2, x]
        xs = []
        for xn in (x - 1, x + 1):
            if 0 <= xn < NX:
                b = 0.5 * (c + fields[0, xn])
                diag = diag + b
                xs.append((xn, b))
        sides = []
        for shift, axis, end, at in ((NY - 1, 0, NY - 1, yi), (1, 0, 0, yi), (NZ - 1, 1, NZ - 1, zi), (1, 1, 0, zi)):
            outside = at == end
            b = jnp.where(outside, c, 0.5 * (c + pltpu.roll(c, shift, axis)))
            diag = diag + b
            sides.append((shift, axis, jnp.where(outside, 0.0, b)))

        def one(i, x=x, diag=diag, damp=damp, xs=xs, sides=sides):
            v = v_ref[i, x]
            f = diag * v + damp * comp_ref[i, x]
            for xn, b in xs:
                f = f - b * v_ref[i, xn]
            for shift, axis, b in sides:
                f = f - b * pltpu.roll(v, shift, axis)
            return f

        if x in (0, NX - 1):
            for i in range(NV):
                edge_ref[x // (NX - 1), i] = one(i)
            continue
        for i in range(0, NV, 2):
            f0, f1 = one(i), one(i + 1)
            for h in range(2):
                at = 2 * (x - 1) + h
                cols, half = slice(at * NZ, (at + 1) * NZ), slice(8 * h, 8 * h + 8)
                high, low = two_parts(jnp.concatenate([f0[half], f1[half]], axis=0))
                xf_ref[8 * i : 8 * i + 16, cols] = high
                xf_ref[128 + 8 * i : 144 + 8 * i, cols] = low
    inner, ends = slice(2 * NZ, 14 * NZ), (slice(0, 2 * NZ), slice(14 * NZ, 16 * NZ))
    high, low = (jnp.concatenate([xf_ref[k : k + 128], xv_ref[k : k + 128, inner]], axis=0) for k in (0, 128))
    end_high, end_low = (jnp.concatenate([xv_ref[k : k + 128, e] for e in ends], axis=1) for k in (0, 128))
    same, mixed = (
        folded(times_turned(high, right)) + beside(folded(times_turned(end_high, end_right)))
        for right, end_right in ((high, end_high), (low, end_low))
    )
    both = same + mixed
    group, lane = iota((32, 128), 0), iota((32, 128), 1)
    over_f, over_v = (
        tiled(both[:, 128 * k : 128 * k + 128])
        + jnp.sum(picked(mixed, group - NV * k == lane % NV, ((0,), (0,))).reshape(32, 8, 128), axis=1)
        for k in (0, 1)
    )
    tiles_ref[0:NV] = over_f[0:NV]
    tiles_ref[NV : NV + 32] = over_v


def main(basis, fields, companion):
    return pl.pallas_call(
        main_kernel,
        out_shape=(
            jax.ShapeDtypeStruct((256, 1536), BF16),
            jax.ShapeDtypeStruct((256, 2048), BF16),
            jax.ShapeDtypeStruct((2, NV, NY, NZ), F32),
            jax.ShapeDtypeStruct((48, 128), F32),
        ),
        in_specs=[VMEM] * 3,
        out_specs=(VMEM,) * 4,
        compiler_params=pltpu.CompilerParams(vmem_limit_bytes=16 << 20),
        cost_estimate=pl.CostEstimate(flops=1 << 28, bytes_accessed=5 << 20, transcendentals=0),
        name="main",
    )(basis, fields, companion)


def edge_kernel(core, edge_ref, tiles_ref, xv_ref, own0, own1, got0, got1, xf_ref, xe_ref, out_ref, kept_ref):
    upper = (core[0], 1 - core[0])
    for side, (own, got) in enumerate(((own0, got0), (own1, got1))):
        place = upper[side]
        c, other = own[NV], got[NV]
        b = 0.5 * (c + jnp.where(other > 0.0, other, c))
        for i in range(0, NV, 2):
            f0, f1 = (edge_ref[place, k] + b * (own[k] - got[k]) for k in (i, i + 1))
            for h in range(2):
                cols, half = pl.ds(pl.multiple_of((place * 2 + h) * NZ, NZ), NZ), slice(8 * h, 8 * h + 8)
                high, low = two_parts(jnp.concatenate([f0[half], f1[half]], axis=0))
                xe_ref[8 * i : 8 * i + 16, cols] = high
                xe_ref[128 + 8 * i : 144 + 8 * i, cols] = low
    fh, fl = xe_ref[0:128], xe_ref[128:256]
    ends = (slice(0, 2 * NZ), slice(14 * NZ, 16 * NZ))
    vh, vl = (jnp.concatenate([xv_ref[k : k + 128, e] for e in ends], axis=1) for k in (0, 128))
    sums = folded(products(fh, fl, jnp.concatenate([fh, vh], axis=0), jnp.concatenate([fl, vl], axis=0)))
    over = tiled(jnp.concatenate([sums[:, 0:128], sums[:, 128:256]], axis=0)) + tiles_ref[0:32]
    ff, fv = over[0:NV], over[NV:32]
    vv = tiles_ref[32:48]
    row, lane = iota((NV, 128), 0), iota((NV, 128), 1)
    sums = []
    for m in (fv, jnp.where(lane % NV >= row, ff, vv)):
        m = jnp.where(lane // NV == row % 8, m, 0.0)
        sums += [jnp.sum(m[0:8], axis=0, keepdims=True), jnp.sum(m[8:16], axis=0, keepdims=True)]
    sums.append(jnp.sum(jnp.where(lane == row, vv, 0.0), axis=0, keepdims=True))
    for k, m in enumerate(sums):
        out_ref[k : k + 1] = m * (1.0 / CELLS)


def edge(core, edges, tiles, xv, own, got, xf):
    anywhere = pl.BlockSpec(memory_space=pl.ANY)
    return pl.pallas_call(
        edge_kernel,
        out_shape=(
            jax.ShapeDtypeStruct((256, 512), BF16),
            jax.ShapeDtypeStruct((5, 128), F32),
            jax.ShapeDtypeStruct(xf.shape, xf.dtype),
        ),
        in_specs=[SMEM] + [VMEM] * 7 + [anywhere],
        out_specs=(VMEM, VMEM, anywhere),
        input_output_aliases={8: 2},
        compiler_params=pltpu.CompilerParams(vmem_limit_bytes=8 << 20),
        cost_estimate=pl.CostEstimate(flops=1 << 27, bytes_accessed=2 << 20, transcendentals=0),
        name="edge",
    )(core, edges, tiles, xv, *own, *got, xf)


def summed(left, right):
    terms = [left[:, k : k + 1] * right[k : k + 1] for k in range(NV)]
    while len(terms) > 1:
        terms = [a + b for a, b in zip(terms[::2], terms[1::2])]
    return terms[0]


def finish_kernel(parts_ref, xf_ref, xe_ref, xv_ref, new_ref, proj_ref, r_ref, stage, sems):
    row, lane = iota((NV, 128), 0), iota((NV, 128), 1)
    total = [jnp.sum(parts_ref[pl.ds(k, parts_ref.shape[0] // 5, stride=5), :], axis=0, keepdims=True) for k in range(5)]
    mine = lane // NV == row % 8
    spread_out = [
        jnp.where(mine, jnp.where(row < 8, jnp.broadcast_to(lo, (NV, 128)), jnp.broadcast_to(hi, (NV, 128))), 0.0)
        for lo, hi in ((total[0], total[1]), (total[2], total[3]))
    ]
    spread_out = jnp.concatenate(spread_out, axis=0)
    source, target = iota((128, 128), 0), iota((128, 128), 1)
    squares = picked(spread_out, (source % NV == target % NV) & (target // NV % 2 == 0) & (target < 48))
    turned = picked(spread_out, lane % NV == row, ((1,), (1,)), values_first=False)
    fv, mixed = squares[0:NV, 0:NV], squares[NV:32, 0:NV]
    vf, mixed_t = turned[:, 0:NV], turned[:, NV:32]
    r, c = iota((NV, NV), 0), iota((NV, NV), 1)
    ff = jnp.where(c >= r, mixed, mixed_t)
    own = jnp.broadcast_to(total[4], (NV, 128))[:, 0:NV]
    vv = jnp.where(c < r, mixed, jnp.where(c > r, mixed_t, own))
    proj_ref[...] = vf
    gram = ff + summed(fv, summed(vv, vf) - 2.0 * vf)
    unit = ones_where(row + 16 == lane)
    a = jnp.pad(gram, ((0, 0), (0, 112))) + unit + jnp.where(lane >= 32, squares[0:NV], 0.0)
    columns = [jnp.broadcast_to(a[:, j : j + 1], (NV, 128)) for j in range(NV)]
    copies = []
    for k in range(0, NV, 2):
        col0, col1 = columns[k : k + 2]
        if k < NV - 2:
            at0, at1 = ({j: jnp.broadcast_to(m[j : j + 1], (NV, 128)) for j in range(k, NV)} for m in (col0, col1))
            p, q, t = at0[k], at1[k], at1[k + 1]
            scale = jnp.where(row > k + 1, 1.0 / (p * t - q * q), 0.0)
            step0, step1 = (col0 * t - col1 * q) * scale, (col1 * p - col0 * q) * scale
            row0, row1 = (jnp.broadcast_to(a[k + j : k + j + 1], (NV, 128)) for j in (0, 1))
            for j in range(k + 2, NV):
                columns[j] = columns[j] - step0 * at0[j] - step1 * at1[j]
            a = a - step0 * row0 - step1 * row1
    high, low = rows_done(a, r_ref)
    for x in range(NX):
        got = spread(xf_ref, xe_ref, xv_ref, high, low, x)
        for h in range(2):
            stage[:, x, 8 * h : 8 * h + 8, :] = got[:, NZ * h : NZ * h + NZ].reshape(NV, 8, NZ)
        if x % 1 == 1-1:
            at = (slice(None), pl.ds(x - 1 + 1, 1))
            copies.append(pltpu.make_async_copy(stage.at[at], new_ref.at[at], sems.at[x // 1]))
            copies[-1].start()
    for copy in copies:
        copy.wait()


def rows_done(a, r_ref):
    row, lane = iota((NV, 128), 0), iota((NV, 128), 1)
    above = pltpu.roll(a, 1, 0)
    before, pivot = (jnp.sum(jnp.where(lane == row - 1, m, 0.0), axis=1, keepdims=True) for m in (a, above))
    odd = row % 2 == 1
    a = a - jnp.where(odd, before / jnp.where(odd[:, 0:1], pivot, 1.0), 0.0) * above
    pivots = jnp.sum(jnp.where(row == lane, a, 0.0), axis=1, keepdims=True)
    a = a / jnp.sqrt(pivots)
    r_ref[...] = jnp.where(lane >= row, a, 0.0)[:, 0:NV]
    w = jnp.where(lane < 32, a, -a)
    w = jnp.broadcast_to(w[:, None, :], (NV, 8, 128)).reshape(128, 128)
    source, target = iota((128, 256), 0), iota((128, 256), 1)
    widen = jnp.where(source - 16 == target // 8, 1.0, 0.0).astype(BF16)
    keep = iota((128, 256), 0) % 8 == iota((128, 256), 1) % 8
    return [
        jnp.where(keep, jnp.dot(part, widen, preferred_element_type=F32), 0.0).astype(BF16) for part in two_parts(w)
    ]


def spread(xf_ref, xe_ref, xv_ref, high, low, x):
    if x in (0, NX - 1):
        f_ref, at = xe_ref, x // (NX - 1)
    else:
        f_ref, at = xf_ref, x - 1
    f_cols, v_cols = slice(256 * at, 256 * at + 256), slice(256 * x, 256 * x + 256)
    fh, fl = f_ref[0:128, f_cols], f_ref[128:256, f_cols]
    vh, vl = xv_ref[0:128, v_cols], xv_ref[128:256, v_cols]
    left = jnp.concatenate([high, high, low], axis=1)
    return jnp.dot(left, jnp.concatenate([fh, vh, fl, vl, fh, vh], axis=0), preferred_element_type=F32)


def finish(parts, xf, xe, xv):
    return pl.pallas_call(
        finish_kernel,
        out_shape=(
            jax.ShapeDtypeStruct((NV, NX, NY, NZ), F32),
            jax.ShapeDtypeStruct((NV, NV), F32),
            jax.ShapeDtypeStruct((NV, NV), F32),
        ),
        in_specs=[VMEM] * 4,
        out_specs=(pl.BlockSpec(memory_space=pl.ANY), VMEM, VMEM),
        scratch_shapes=[pltpu.VMEM((NV, NX, NY, NZ), F32), pltpu.SemaphoreType.DMA((NX,))],
        compiler_params=pltpu.CompilerParams(vmem_limit_bytes=16 << 20),
        cost_estimate=pl.CostEstimate(flops=1 << 29, bytes_accessed=3 << 20, transcendentals=0),
        name="finish",
    )(parts, xf, xe, xv)


def sent_to_all(x, axes):
    peers = lax.axis_size(axes)
    return lax.all_to_all(jnp.broadcast_to(x[None], (peers, *x.shape)), axes, 0, 0, tiled=True)


def shards(krylov_basis_block, companion, region, inv_density, stiffness, damping):
    core = lax.axis_index("slab_3").astype(jnp.int32).reshape(1)
    count = lax.axis_size(SLAB)
    *own, fields = pack(core, inv_density, stiffness, damping, krylov_basis_block, region)
    own[0] = hold(own[0], krylov_basis_block, companion)
    pairs = [(i, i ^ 1) for i in range(count)]
    across = [(i, i + 1 if i % 2 else i - 1) for i in range(1, count - 1)]
    got0 = lax.ppermute(own[0], SLAB, across)
    got1 = lax.ppermute(own[1], SLAB, pairs)
    xf, xv, edges, tiles = main(krylov_basis_block, fields, companion)
    xe, packed, xf = edge(core, edges, tiles, xv, own, (got0, got1), xf)
    near = sent_to_all(packed.reshape(1, 640), ("slab_2", "slab_3")).sum(axis=0)
    far = sent_to_all(near.reshape(1, 640), ("slab_0", "slab_1"))
    new_block, projection, rfactor = finish(far.reshape(-1, 128), xf, xe, xv)
    return new_block, projection, rfactor


def solution(mesh):
    torus = Mesh(mesh.devices.reshape(8, 4, 8, 2), SLAB)
    placed = (
        P(None, SLAB, None, None),
        P(None, SLAB, None, None),
        P(SLAB, None, None),
        P(),
        P(),
        P(),
    )
    return jax.shard_map(
        shards,
        mesh=torus,
        in_specs=placed,
        out_specs=(P(None, SLAB, None, None), P(), P()),
        check_vma=False,
    )
```
